32 devices in a mesh: grp: 2 (over x), src: 8 (over z, y), tgt: 2 (over core).
Axes of the slice: x: 2, y: 2, z: 4, core: 2. Of those that a mesh axis runs over, the one named last changes fastest.
Arguments:
- densities: bfloat16 [512, 32768], P('grp', ('src', 'tgt')), parts along dimension 0, may hold values from -6 to 6
- compress: bfloat16 [65536, 2, 256], P(('grp', 'src', 'tgt')), parts along dimension 0, may hold values from -0.0625 to 0.0625
- level_a: bfloat16 [6, 2048, 2, 256], P('grp', 'src', None, 'tgt'), parts along dimension 0, may hold values from -0.1875 to 0.1875
- level_b: bfloat16 [6, 2048, 2, 256], P('grp', 'src', None, 'tgt'), parts along dimension 0, may hold values from -0.1875 to 0.1875
- expand: bfloat16 [4096, 2, 4096], P(('grp', 'src'), None, 'tgt'), parts along dimension 0, may hold values from -0.25 to 0.25
- near_tiles: bfloat16 [2048, 128, 2, 128], P(('grp', 'src', 'tgt')), parts along dimension 0, may hold values from -0.375 to 0.375
- tile_pairs: int32 [2048, 2], P(('grp', 'src', 'tgt')), parts along dimension 0, may hold values from 0 to 15
- tile_count: int32 [32], P(('grp', 'src', 'tgt')), parts along dimension 0, may hold values from 1 to 63, as said below
- cluster_order: int32 [32, 16], P(('grp', 'src', 'tgt')), parts along dimension 0, may hold values from 0 to 15, each once within a row
Outputs:
- potential: bfloat16 [512, 32768], P('grp', ('src', 'tgt')), parts along dimension 0
The draws below stay inside these ranges and needn't reach their ends.
There are 2 independent parts, one for each index of `grp`. The reference program is written for one: setup_inputs(seed, part) draws one part's arguments, and reference() takes and returns one part's arrays. A program takes and returns all parts, laid end to end along the dimension named above; each array names one. Nothing has to cross between parts.
Inputs may be any that keep to these rules, and one draw needn't show every extreme that they name: For every i below 8, tile_count[i] + tile_count[i + 8] == 64; slots at or beyond a device's count are unused. `cluster_order`: each row is a permutation.
All inputs are finite; a program needn't handle non-finite values.
Results may differ from the reference program's by a relative error of at most 0.007.
Values may be sent and summed in bfloat16 or wider, within the bound.
No kernel may reach another device: no remote copies, remote signals or barrier semaphores. Data moves between devices by JAX's collectives and lax.ppermute only.
A program may use at most 128 MiB of HBM per device.

```python
import jax
import jax.numpy as jnp
from jax import lax

RHS = 128
K = 256
PC = 128
MAXT = 64
PTS = 2048
CL = 16
SHARDS = 16
PTS_ALL = 32768
LEVELS = 3
N_SRC = 8
N_TGT = 2


def draw_tile_count(key, part):
    src_total = SHARDS // N_TGT
    halfway = src_total // 2
    first_key, second_key = jax.random.split(jax.random.fold_in(key, 17))
    heavy = jax.random.randint(first_key, (halfway, N_TGT), MAXT // 2, MAXT)
    heavy = heavy.at[0, 0].set(MAXT - 1)
    light = MAXT - heavy
    flipped = jax.random.randint(second_key, (halfway, N_TGT), 0, 2)
    lower = jnp.where(flipped == 1, heavy, light)
    upper = jnp.where(flipped == 1, light, heavy)
    return jnp.concatenate([lower, upper], axis=0).reshape(SHARDS).astype(jnp.int32)


def set_ends(drawn, rng, low, top_value):
    dims = drawn.shape
    spot = [jax.random.randint(jax.random.fold_in(rng, axis), (), 0, dims[axis]) for axis in range(len(dims))]
    drawn = drawn.at[tuple(spot)].set(low)
    longest = dims.index(max(dims))
    spot[longest] = (spot[longest] + 1) % dims[longest]
    return drawn.at[tuple(spot)].set(top_value)


def level_of(key, shape, cuts, least, largest):
    factor_of, own = 1.0, jax.random.fold_in(key, 6)
    for axis_at, shards_of in cuts:
        heights = jnp.exp(jax.random.uniform(jax.random.fold_in(own, axis_at), (shards_of,), jnp.float32, least / len(cuts), largest / len(cuts)))
        factor_of = factor_of * jnp.repeat(heights, shape[axis_at] // shards_of).reshape([-1 if axis == axis_at else 1 for axis in range(len(shape))])
    return factor_of


def gaussian(key, extent, scale, limit, cuts=(), held_as=jnp.bfloat16):
    gain = level_of(key, extent, cuts, -0.22, 0.18) if cuts else 1.0
    result = jax.random.normal(key, extent, jnp.float32) * scale * gain
    return jnp.minimum(jnp.maximum(result, -limit), limit).astype(held_as)


def setup_inputs(seed: int = 0, part: int = 0) -> dict:
    key_of = jax.random.split(jax.random.key(seed), 10)
    part_splits = jax.random.split(jax.random.fold_in(key_of[9], part), 10)
    return {
        "densities": gaussian(part_splits[0], (2 * RHS, PTS_ALL), 1.0, 6.0, ((1, 16),)),
        "compress": gaussian(part_splits[1], (PTS_ALL, 2, K), (2 * N_TGT * PTS) ** -0.5, 0.0625, ((0, 16),)),
        "level_a": gaussian(part_splits[2], (LEVELS, N_SRC * K, 2, K), (4 * K) ** -0.5, 0.1875, ((1, 8), (3, 2))),
        "level_b": gaussian(part_splits[3], (LEVELS, N_SRC * K, 2, K), (4 * K) ** -0.5, 0.1875, ((1, 8), (3, 2))),
        "expand": gaussian(part_splits[4], (N_SRC * K, 2, N_TGT * PTS), (2 * K) ** -0.5, 0.25, ((0, 8), (2, 2))),
        "near_tiles": gaussian(part_splits[5], (SHARDS * MAXT, PC, 2, PC), (2 * PC) ** -0.5, 0.375, ((0, 16),)),
        "tile_pairs": set_ends(jax.random.randint(part_splits[6], (SHARDS * MAXT, 2), 0, CL), jax.random.fold_in(part_splits[6], 1), 0, CL - 1).astype(jnp.int32),
        "tile_count": draw_tile_count(jax.random.fold_in(jax.random.fold_in(key_of[9], part), 71), part),
        "cluster_order": jax.vmap(lambda own: jax.random.permutation(own, CL))(jax.random.split(part_splits[8], SHARDS)).reshape((SHARDS, CL)).astype(jnp.int32),
    }


def complex_product(operand, matrix):
    product = jnp.dot(operand, matrix, preferred_element_type=jnp.float32)
    half_rows = operand.shape[0] // 2
    half_cols = matrix.shape[1] // 2
    real_part = product[:half_rows, :half_cols] - product[half_rows:, half_cols:]
    imag_part = product[:half_rows, half_cols:] + product[half_rows:, :half_cols]
    return jnp.concatenate([real_part, imag_part], axis=0)


def near_sum(sources, tile_blocks, source_ids, target_ids, active, targets):
    half_rows = sources.shape[0] // 2
    cluster_size = tile_blocks.shape[1]
    picked = jnp.take(sources, source_ids, axis=1).astype(jnp.float32)
    product = jnp.einsum("rjp,jpq->rjq", picked, tile_blocks.astype(jnp.float32), precision=lax.Precision.HIGHEST)
    real_part = product[:half_rows, :, :cluster_size] - product[half_rows:, :, cluster_size:]
    imag_part = product[:half_rows, :, cluster_size:] + product[half_rows:, :, :cluster_size]
    joined = jnp.concatenate([real_part, imag_part], axis=0)
    chooser = ((target_ids[:, None] == jnp.arange(targets, dtype=jnp.int32)[None, :]) & active[:, None]).astype(jnp.float32)
    return jnp.einsum("rjq,jc->rcq", joined, chooser, precision=lax.Precision.HIGHEST)


def reference(densities, compress, level_a, level_b, expand, near_tiles, tile_pairs, tile_count, cluster_order):
    row_count = densities.shape[0]
    shard_dens = densities.reshape(row_count, SHARDS, PTS).transpose(1, 0, 2)
    shard_comp = compress.reshape(SHARDS, PTS, 2 * K)

    def compress_one(items):
        return complex_product(items[0], items[1])

    partial_value = lax.map(compress_one, (shard_dens, shard_comp))
    coefficients = jnp.sum(partial_value.reshape(N_SRC, N_TGT, row_count, K), axis=1).astype(jnp.bfloat16)
    full_a = level_a.reshape(LEVELS, N_SRC, K, 2 * K)
    full_b = level_b.reshape(LEVELS, N_SRC, K, 2 * K)

    def level_one(items):
        summed = complex_product(items[0], items[2]) + complex_product(items[1], items[3])
        return summed.astype(jnp.bfloat16)

    for level_index in range(LEVELS):
        partner_index = jnp.bitwise_xor(jnp.arange(N_SRC, dtype=jnp.int32), 1 << level_index)
        partner_coeff = coefficients[partner_index]
        coefficients = lax.map(level_one, (coefficients, partner_coeff, full_a[level_index], full_b[level_index]))

    shard_coeff = jnp.repeat(coefficients, N_TGT, axis=0)
    shard_expand = expand.reshape(N_SRC, K, 2, N_TGT, PTS).transpose(0, 3, 1, 2, 4).reshape(SHARDS, K, 2 * PTS)
    shard_tiles = near_tiles.reshape(SHARDS, MAXT, PC, 2 * PC)
    shard_pairs = tile_pairs.reshape(SHARDS, MAXT, 2)

    def finish_one(items):
        dens, coeff, expansion, tile_blocks, pairs, count, order = items
        far_field = complex_product(coeff, expansion).reshape(row_count, CL, PC)
        placed = jnp.zeros((row_count, CL, PC), jnp.float32).at[:, order, :].set(far_field)
        active = jnp.arange(MAXT, dtype=jnp.int32) < count
        near_field = near_sum(dens.reshape(row_count, CL, PC), tile_blocks, pairs[:, 1], pairs[:, 0], active, CL)
        return (placed + near_field).reshape(row_count, PTS).astype(jnp.bfloat16)

    results = lax.map(finish_one, (shard_dens, shard_coeff, shard_expand, shard_tiles, shard_pairs, tile_count, cluster_order))
    return results.transpose(1, 0, 2).reshape(row_count, PTS_ALL)
```

```python
import functools

import jax
import jax.numpy as jnp
from jax import lax
from jax.experimental import pallas as pl
from jax.experimental.pallas import tpu as pltpu
from jax.sharding import PartitionSpec as P

VMEM = pltpu.VMEM
CHUNKS = 4
NEAR_CALLS = 3
UNROLL = 4


def in_vmem():
    return pl.BlockSpec(memory_space=pltpu.VMEM)


def in_smem():
    return pl.BlockSpec(memory_space=pltpu.SMEM)


def in_hbm():
    return pl.BlockSpec(memory_space=pltpu.HBM)


def swapped(value, axis, bit):
    mask = 2**bit
    pairs = [(source, source ^ mask) for source in range(lax.axis_size(axis))]
    return lax.ppermute(value, axis, pairs)


def paired(block):
    half = block.shape[0] // 2
    upper, lower = block[:half], block[half:]
    return jnp.concatenate(
        [jnp.concatenate([upper, -lower], axis=1), jnp.concatenate([lower, upper], axis=1)], axis=0
    )


def compress_kernel(clusters, core_ref, dens_hbm, comp_hbm, mixed_ref, keep_ref, send_ref, dens, comp, weave, total, sems):
    rows, points = dens.shape
    width = points // clusters
    rank = comp.shape[1]
    comp_flat = comp_hbm.reshape(2 * points, rank)
    step = points // CHUNKS
    copies = []
    for chunk in range(CHUNKS):
        columns = pl.ds(chunk * step, step)
        planes = pl.ds(2 * chunk * step, 2 * step)
        pair = (
            pltpu.make_async_copy(dens_hbm.at[:, columns], dens.at[:, columns], sems.at[chunk, 0]),
            pltpu.make_async_copy(comp_flat.at[planes, :], comp.at[planes, :], sems.at[chunk, 1]),
        )
        for copy in pair:
            copy.start()
        copies.append(pair)
    row_id = lax.broadcasted_iota(jnp.int32, (2 * width, 2 * width), 0)
    col_id = lax.broadcasted_iota(jnp.int32, (2 * width, 2 * width), 1)
    goal = jnp.where(row_id < width, 2 * row_id, 2 * (row_id - width) + 1)
    weave[...] = jnp.where(col_id == goal, 1.0, 0.0).astype(jnp.bfloat16)
    for chunk in range(CHUNKS):
        copies[chunk][0].wait()
        pieces = []
        for cluster in range(chunk * clusters // CHUNKS, (chunk + 1) * clusters // CHUNKS):
            block = paired(dens[:, cluster * width : (cluster + 1) * width])
            woven = jnp.dot(block, weave[...], preferred_element_type=jnp.float32).astype(jnp.bfloat16)
            mixed_ref[cluster] = woven
            pieces.append(woven)
        copies[chunk][1].wait()
        product = jnp.dot(
            jnp.concatenate(pieces, axis=1),
            comp[2 * chunk * step : 2 * (chunk + 1) * step, :],
            preferred_element_type=jnp.float32,
        )
        if chunk == 0:
            total[...] = product
        else:
            total[...] += product
    quarter = rows // 4
    core = core_ref[0]
    for part in range(2):
        mine = pl.ds(pl.multiple_of(2 * part * quarter + core * quarter, quarter), quarter)
        other = pl.ds(pl.multiple_of(2 * part * quarter + (1 - core) * quarter, quarter), quarter)
        keep_ref[part * quarter : (part + 1) * quarter, :] = total[mine, :]
        send_ref[part * quarter : (part + 1) * quarter, :] = total[other, :].astype(jnp.bfloat16)


def compress_call(core, densities, compress, clusters):
    rows, points = densities.shape
    rank = compress.shape[2]
    width = points // clusters
    return pl.pallas_call(
        functools.partial(compress_kernel, clusters),
        out_shape=(
            jax.ShapeDtypeStruct((clusters, rows, 2 * width), jnp.bfloat16),
            jax.ShapeDtypeStruct((rows // 2, rank), jnp.float32),
            jax.ShapeDtypeStruct((rows // 2, rank), jnp.bfloat16),
        ),
        in_specs=[in_smem(), in_hbm(), in_hbm()],
        out_specs=(in_vmem(), in_vmem(), in_vmem()),
        scratch_shapes=[
            VMEM((rows, points), jnp.bfloat16),
            VMEM((2 * points, rank), jnp.bfloat16),
            VMEM((2 * width, 2 * width), jnp.bfloat16),
            VMEM((rows, rank), jnp.float32),
            pltpu.SemaphoreType.DMA((CHUNKS, 2)),
        ],
        compiler_params=pltpu.CompilerParams(vmem_limit_bytes=16 << 20),
        name="compress",
    )(core, densities, compress)


def near_kernel(call, pairs_ref, count_ref, mixed_ref, tiles_ref, *refs):
    total = refs[-1]
    if call == 0:
        total[...] = jnp.zeros_like(total)
    clusters = total.shape[0] - 1
    slots = tiles_ref.shape[0]
    count = count_ref[0]
    first = (count * call) // NEAR_CALLS
    last = (count * (call + 1)) // NEAR_CALLS

    def body(trip, carry):
        base = first + trip * UNROLL
        for lane in range(UNROLL):
            slot = jnp.minimum(base + lane, slots - 1)
            target = jnp.where(base + lane < last, pairs_ref[slot, 0], clusters)
            total[target] += jnp.dot(
                mixed_ref[pairs_ref[slot, 1]], tiles_ref[slot], preferred_element_type=jnp.float32
            )
        return carry

    lax.fori_loop(0, (last - first + UNROLL - 1) // UNROLL, body, 0)


def near_call(call, pairs, count, mixed, tiles, total):
    clusters, rows, depth = mixed.shape
    width = tiles.shape[2]
    operands = [pairs, count, mixed, tiles]
    specs = [in_smem(), in_smem(), in_vmem(), in_vmem()]
    aliases = {}
    if total is not None:
        operands.append(total)
        specs.append(in_vmem())
        aliases = {4: 0}
    return pl.pallas_call(
        functools.partial(near_kernel, call),
        out_shape=jax.ShapeDtypeStruct((clusters + 1, rows, width), jnp.float32),
        in_specs=specs,
        out_specs=in_vmem(),
        input_output_aliases=aliases,
        cost_estimate=pl.CostEstimate(
            flops=2 * rows * depth * width * tiles.shape[0] // NEAR_CALLS, bytes_accessed=0, transcendentals=0
        ),
        compiler_params=pltpu.CompilerParams(vmem_limit_bytes=16 << 20),
        name=f"near{call}",
    )(*operands)


def expand_kernel(half_ref, order_ref, coeff_ref, matrix_ref, near_ref, *refs):
    out_hbm, rows_out, inverse, sems = refs[-4:]
    clusters = order_ref.shape[1]
    points = matrix_ref.shape[1]
    width = points // clusters
    rows = near_ref.shape[1]
    quarter = rows // 4
    half = half_ref[0]

    def note(cluster, carry):
        inverse[order_ref[0, cluster]] = cluster
        return carry

    lax.fori_loop(0, clusters, note, 0)
    lhs = paired(coeff_ref[...])
    group = clusters // CHUNKS
    copies = []
    for chunk in range(CHUNKS):
        blocks = []
        for place in range(chunk * group, (chunk + 1) * group):
            start = pl.multiple_of(inverse[place] * width, width)
            blocks.append(matrix_ref[:, pl.ds(start, width)])
        far = jnp.dot(lhs, jnp.concatenate(blocks, axis=1), preferred_element_type=jnp.float32)
        for part in range(2):
            source = pl.ds(pl.multiple_of(2 * part * quarter + half * quarter, quarter), quarter)
            for item in range(group):
                place = chunk * group + item
                value = far[part * quarter : (part + 1) * quarter, item * width : (item + 1) * width]
                rows_out[part * quarter : (part + 1) * quarter, place * width : (place + 1) * width] = (
                    value + near_ref[place, source, :]
                ).astype(jnp.bfloat16)
            columns = pl.ds(chunk * group * width, group * width)
            copy = pltpu.make_async_copy(
                rows_out.at[part * quarter : (part + 1) * quarter, columns],
                out_hbm.at[source, columns],
                sems.at[chunk, part],
            )
            copy.start()
            copies.append(copy)
    for copy in copies:
        copy.wait()


def expand_call(half, order, coefficients, matrix, near, result):
    clusters = order.shape[1]
    points = matrix.shape[1]
    rows = near.shape[1]
    operands = [half, order, coefficients, matrix, near]
    specs = [in_smem(), in_smem(), in_vmem(), in_vmem(), in_vmem()]
    aliases = {}
    if result is not None:
        operands.append(result)
        specs.append(in_hbm())
        aliases = {5: 0}
    return pl.pallas_call(
        expand_kernel,
        out_shape=jax.ShapeDtypeStruct((rows, points), jnp.bfloat16),
        in_specs=specs,
        out_specs=in_hbm(),
        input_output_aliases=aliases,
        scratch_shapes=[
            VMEM((rows // 2, points), jnp.bfloat16),
            pltpu.SMEM((clusters,), jnp.int32),
            pltpu.SemaphoreType.DMA((CHUNKS, 2)),
        ],
        compiler_params=pltpu.CompilerParams(vmem_limit_bytes=16 << 20),
        name="expand",
    )(*operands)


def shards(
    densities, compress, level_a, level_b, expand, near_tiles, tile_pairs, tile_count, cluster_order
):
    rows, points = densities.shape
    rank = compress.shape[2]
    sections = level_a.shape[0]
    clusters = cluster_order.shape[1]
    width = points // clusters
    slots = near_tiles.shape[0]
    core = lax.axis_index("tgt").astype(jnp.int32)
    mine = core.reshape(1)
    tiles = near_tiles.reshape(slots, 2 * width, width)

    mixed, keep, send = compress_call(mine, densities, compress, clusters)
    arrived = swapped(send, "tgt", 0)
    coefficients = (keep + arrived.astype(jnp.float32)).astype(jnp.bfloat16)

    def whole(matrix):
        other = swapped(matrix, "tgt", 0)
        first = jnp.where(core == 0, matrix, other)
        second = jnp.where(core == 0, other, matrix)
        joined = jnp.concatenate([first, second], axis=3)
        return joined.transpose(0, 2, 1, 3).reshape(sections, 2 * rank, rank)

    own_matrices, partner_matrices = whole(level_a), whole(level_b)
    matrix = expand.transpose(1, 0, 2).reshape(2 * rank, points)
    near = None
    for section in range(sections):
        partner = swapped(coefficients, "src", section)
        if section < NEAR_CALLS:
            near = near_call(section, tile_pairs, tile_count, mixed, tiles, near)
        updated = jnp.dot(
            paired(coefficients), own_matrices[section], preferred_element_type=jnp.float32
        ) + jnp.dot(paired(partner), partner_matrices[section], preferred_element_type=jnp.float32)
        coefficients = updated.astype(jnp.bfloat16)
    others = swapped(coefficients, "tgt", 0)
    result = expand_call(mine, cluster_order, coefficients, matrix, near, None)
    return expand_call(1 - mine, cluster_order, others, matrix, near, result)


def solution(mesh):
    placed = (
        P("grp", ("src", "tgt")),
        P(("grp", "src", "tgt"), None, None),
        P("grp", "src", None, "tgt"),
        P("grp", "src", None, "tgt"),
        P(("grp", "src"), None, "tgt"),
        P(("grp", "src", "tgt"), None, None, None),
        P(("grp", "src", "tgt"), None),
        P(("grp", "src", "tgt")),
        P(("grp", "src", "tgt"), None),
    )
    return jax.shard_map(
        shards, mesh=mesh, in_specs=placed, out_specs=P("grp", ("src", "tgt")), check_vma=False
    )
```

```python
import functools

import jax
import jax.numpy as jnp
from jax import lax
from jax.experimental import pallas as pl
from jax.experimental.pallas import tpu as pltpu
from jax.sharding import PartitionSpec as P


VMEM = pltpu.VMEM
CHUNKS = 4
NEAR_CALLS = 3
UNROLL = 8


def in_vmem():
    return pl.BlockSpec(memory_space=pltpu.VMEM)


def in_smem():
    return pl.BlockSpec(memory_space=pltpu.SMEM)


def in_hbm():
    return pl.BlockSpec(memory_space=pltpu.HBM)


def swapped(value, axis, bit):
    mask = 2**bit
    pairs = [(source, source ^ mask) for source in range(lax.axis_size(axis))]
    return lax.ppermute(value, axis, pairs)


def paired(block):
    half = block.shape[0] // 2
    upper, lower = block[:half], block[half:]
    return jnp.concatenate(
        [jnp.concatenate([upper, -lower], axis=1), jnp.concatenate([lower, upper], axis=1)], axis=0
    )


def weave_kernel(dens_ref, mixed_ref, weave):
    clusters = mixed_ref.shape[0]
    width = dens_ref.shape[1] // clusters
    row_id = lax.broadcasted_iota(jnp.int32, (2 * width, 2 * width), 0)
    col_id = lax.broadcasted_iota(jnp.int32, (2 * width, 2 * width), 1)
    goal = jnp.where(row_id < width, 2 * row_id, 2 * (row_id - width) + 1)
    weave[...] = jnp.where(col_id == goal, 1.0, 0.0).astype(jnp.bfloat16)

    def body(trip, carry):
        for lane in range(2):
            cluster = 2 * trip + lane
            block = paired(dens_ref[:, pl.ds(pl.multiple_of(cluster * width, width), width)])
            woven = jnp.dot(block, weave[...], preferred_element_type=jnp.float32)
            mixed_ref[cluster] = woven.astype(jnp.bfloat16)
        return carry

    lax.fori_loop(0, clusters // 2, body, 0)


def weave_call(densities, clusters):
    rows, points = densities.shape
    width = points // clusters
    return pl.pallas_call(
        weave_kernel,
        out_shape=jax.ShapeDtypeStruct((clusters, rows, 2 * width), jnp.bfloat16),
        in_specs=[in_vmem()],
        out_specs=in_vmem(),
        scratch_shapes=[VMEM((2 * width, 2 * width), jnp.bfloat16)],
        cost_estimate=pl.CostEstimate(
            flops=4 * rows * points * width, bytes_accessed=0, transcendentals=0
        ),
        compiler_params=pltpu.CompilerParams(vmem_limit_bytes=16 << 20),
        name="weave",
    )(densities)


def near_kernel(call, pairs_ref, count_ref, mixed_ref, tiles_ref, *refs):
    total = refs[-1]
    if call == 0:
        total[...] = jnp.zeros_like(total)
    clusters = total.shape[0] - 1
    slots = tiles_ref.shape[0]
    count = count_ref[0]
    trips = (count + UNROLL - 1) // UNROLL

    def body(trip, carry):
        for lane in range(UNROLL):
            slot = jnp.minimum(trip * UNROLL + lane, slots - 1)
            target = jnp.where(trip * UNROLL + lane < count, pairs_ref[0, slot], clusters)
            total[target] += jnp.dot(
                mixed_ref[pairs_ref[1, slot]], tiles_ref[slot], preferred_element_type=jnp.float32
            )
        return carry

    lax.fori_loop((trips * call) // NEAR_CALLS, (trips * (call + 1)) // NEAR_CALLS, body, 0)


def near_call(call, pairs, count, mixed, tiles, total):
    clusters, rows, depth = mixed.shape
    width = tiles.shape[2]
    operands = [pairs, count, mixed, tiles]
    specs = [in_smem(), in_smem(), in_vmem(), in_vmem()]
    aliases = {}
    if total is not None:
        operands.append(total)
        specs.append(in_vmem())
        aliases = {4: 0}
    return pl.pallas_call(
        functools.partial(near_kernel, call),
        out_shape=jax.ShapeDtypeStruct((clusters + 1, rows, width), jnp.float32),
        in_specs=specs,
        out_specs=in_vmem(),
        input_output_aliases=aliases,
        cost_estimate=pl.CostEstimate(
            flops=2 * rows * depth * width * tiles.shape[0] // NEAR_CALLS, bytes_accessed=0, transcendentals=0
        ),
        compiler_params=pltpu.CompilerParams(vmem_limit_bytes=16 << 20),
    )(*operands)


def expand_kernel(half_ref, order_ref, coeff_ref, matrix_ref, near_ref, *refs):
    out_hbm, rows_out, inverse, sems = refs[-4:]
    clusters = order_ref.shape[1]
    points = matrix_ref.shape[1]
    width = points // clusters
    rows = near_ref.shape[1]
    quarter = rows // 4
    half = half_ref[0]

    def note(cluster, carry):
        inverse[order_ref[0, cluster]] = cluster
        return carry

    lax.fori_loop(0, clusters, note, 0)
    lhs = paired(coeff_ref[...])
    group = clusters // CHUNKS
    copies = []
    for chunk in range(CHUNKS):
        blocks = []
        for place in range(chunk * group, (chunk + 1) * group):
            start = pl.multiple_of(inverse[place] * width, width)
            blocks.append(matrix_ref[:, pl.ds(start, width)])
        far = jnp.dot(lhs, jnp.concatenate(blocks, axis=1), preferred_element_type=jnp.float32)
        for part in range(2):
            source = pl.ds(pl.multiple_of(2 * part * quarter + half * quarter, quarter), quarter)
            for item in range(group):
                place = chunk * group + item
                value = far[part * quarter : (part + 1) * quarter, item * width : (item + 1) * width]
                rows_out[part * quarter : (part + 1) * quarter, place * width : (place + 1) * width] = (
                    value + near_ref[place, source, :]
                ).astype(jnp.bfloat16)
            columns = pl.ds(chunk * group * width, group * width)
            copy = pltpu.make_async_copy(
                rows_out.at[part * quarter : (part + 1) * quarter, columns],
                out_hbm.at[source, columns],
                sems.at[chunk, part],
            )
            copy.start()
            copies.append(copy)
    for copy in copies:
        copy.wait()


def expand_call(half, order, coefficients, matrix, near, result):
    clusters = order.shape[1]
    points = matrix.shape[1]
    rows = near.shape[1]
    operands = [half, order, coefficients, matrix, near]
    specs = [in_smem(), in_smem(), in_vmem(), in_vmem(), in_vmem()]
    aliases = {}
    if result is not None:
        operands.append(result)
        specs.append(in_hbm())
        aliases = {5: 0}
    return pl.pallas_call(
        expand_kernel,
        out_shape=jax.ShapeDtypeStruct((rows, points), jnp.bfloat16),
        in_specs=specs,
        out_specs=in_hbm(),
        input_output_aliases=aliases,
        scratch_shapes=[
            VMEM((rows // 2, points), jnp.bfloat16),
            pltpu.SMEM((clusters,), jnp.int32),
            pltpu.SemaphoreType.DMA((CHUNKS, 2)),
        ],
        compiler_params=pltpu.CompilerParams(vmem_limit_bytes=16 << 20),
        name="expand",
    )(*operands)


def shards(
    densities, compress, level_a, level_b, expand, near_tiles, tile_pairs, tile_count, cluster_order
):
    rows, points = densities.shape
    rank = compress.shape[2]
    sections = level_a.shape[0]
    clusters = cluster_order.shape[1]
    width = points // clusters
    slots = near_tiles.shape[0]
    core = lax.axis_index("tgt").astype(jnp.int32)
    mine = core.reshape(1)
    tiles = near_tiles.reshape(slots, 2 * width, width)
    pairs = tile_pairs.T
    half_rows = rows // 2

    product = jnp.dot(
        densities, compress.reshape(points, 2 * rank), preferred_element_type=jnp.float32
    )
    upper, lower = product[:half_rows], product[half_rows:]
    quarter = half_rows // 2
    first_core = core == 0
    keep, send = [], []
    for value in (upper[:, :rank] - lower[:, rank:], upper[:, rank:] + lower[:, :rank]):
        keep.append(jnp.where(first_core, value[:quarter], value[quarter:]))
        send.append(jnp.where(first_core, value[quarter:], value[:quarter]))
    keep = jnp.concatenate(keep, axis=0)
    arrived = swapped(jnp.concatenate(send, axis=0).astype(jnp.bfloat16), "tgt", 0)
    mixed = weave_call(densities, clusters)
    coefficients = (keep + arrived.astype(jnp.float32)).astype(jnp.bfloat16)

    def both(matrix):
        planes = matrix.transpose(0, 2, 1, 3)
        joined = jnp.concatenate([planes, swapped(planes, "tgt", 0)], axis=3)
        return joined.reshape(sections, 2 * rank, rank)

    own_matrices, partner_matrices = both(level_a), both(level_b)
    matrix = expand.transpose(1, 0, 2).reshape(2 * rank, points)
    near = None
    for section in range(sections):
        partner = swapped(coefficients, "src", section)
        if section < NEAR_CALLS:
            near = near_call(section, pairs, tile_count, mixed, tiles, near)
        updated = jnp.dot(
            paired(coefficients), own_matrices[section], preferred_element_type=jnp.float32
        ) + jnp.dot(paired(partner), partner_matrices[section], preferred_element_type=jnp.float32)
        updated = updated.astype(jnp.bfloat16)
        turned = jnp.concatenate([updated[:, rank // 2 :], updated[:, : rank // 2]], axis=1)
        coefficients = jnp.where(first_core, updated, turned)
    others = swapped(coefficients, "tgt", 0)
    result = expand_call(mine, cluster_order, coefficients, matrix, near, None)
    return expand_call(1 - mine, cluster_order, others, matrix, near, result)


def solution(mesh):
    placed = (
        P("grp", ("src", "tgt")),
        P(("grp", "src", "tgt"), None, None),
        P("grp", "src", None, "tgt"),
        P("grp", "src", None, "tgt"),
        P(("grp", "src"), None, "tgt"),
        P(("grp", "src", "tgt"), None, None, None),
        P(("grp", "src", "tgt"), None),
        P(("grp", "src", "tgt")),
        P(("grp", "src", "tgt"), None),
    )
    return jax.shard_map(
        shards, mesh=mesh, in_specs=placed, out_specs=P("grp", ("src", "tgt")), check_vma=False
    )
```

```python
import jax
import jax.numpy as jnp
from jax import lax
from jax.experimental import pallas as pl
from jax.experimental.pallas import tpu as pltpu
from jax.sharding import PartitionSpec as P


NEAR_SHARES = (0, 2, 5, 8)
UNROLL = 8


def in_vmem():
    return pl.BlockSpec(memory_space=pltpu.VMEM)


def in_hbm():
    return pl.BlockSpec(memory_space=pltpu.HBM)


def anywhere():
    return pl.BlockSpec(memory_space=pl.ANY)


def swapped(value, axis, bit):
    mask = 2**bit
    pairs = [(source, source ^ mask) for source in range(lax.axis_size(axis))]
    return lax.ppermute(value, axis, pairs)


def paired(block):
    half = block.shape[0] // 2
    upper, lower = block[:half], block[half:]
    return jnp.concatenate(
        [jnp.concatenate([upper, -lower], axis=1), jnp.concatenate([lower, upper], axis=1)], axis=0
    )


def weave_into(mixed_ref, dens_ref, weave):
    clusters = mixed_ref.shape[0]
    width = dens_ref.shape[1] // clusters
    row_id = lax.broadcasted_iota(jnp.int32, (2 * width, 2 * width), 0)
    col_id = lax.broadcasted_iota(jnp.int32, (2 * width, 2 * width), 1)
    goal = jnp.where(row_id < width, 2 * row_id, 2 * (row_id - width) + 1)
    weave[...] = jnp.where(col_id == goal, 1.0, 0.0).astype(jnp.bfloat16)
    lanes = min(UNROLL, clusters)

    def body(trip, carry):
        for lane in range(lanes):
            cluster = lanes * trip + lane
            block = paired(dens_ref[:, pl.ds(pl.multiple_of(cluster * width, width), width)])
            woven = jnp.dot(block, weave[...], preferred_element_type=jnp.float32)
            mixed_ref[cluster] = woven.astype(jnp.bfloat16)
        return carry

    lax.fori_loop(0, clusters // lanes, body, 0)


def bounds(count, call):
    trips = (count + UNROLL - 1) // UNROLL
    return (trips * NEAR_SHARES[call]) // NEAR_SHARES[-1]


def tile_copy(tiles_hbm, tiles_ref, sems, trip):
    span = pl.ds(pl.multiple_of(trip * UNROLL, UNROLL), UNROLL)
    return pltpu.make_async_copy(tiles_hbm.at[span], tiles_ref.at[span], sems.at[trip])


def start_tiles(tiles_hbm, tiles_ref, sems, first, last):
    def body(trip, carry):
        tile_copy(tiles_hbm, tiles_ref, sems, trip).start()
        return carry

    lax.fori_loop(first, last, body, 0)


def wait_tiles(tiles_hbm, tiles_ref, sems, first, last):
    def body(trip, carry):
        tile_copy(tiles_hbm, tiles_ref, sems, trip).wait()
        return carry

    lax.fori_loop(first, last, body, 0)


def add_tiles(first, last, pairs_ref, count, mixed_ref, tiles_ref, total, ready):
    clusters = mixed_ref.shape[0]
    width = tiles_ref.shape[2]

    def body(trip, carry):
        ready(trip)
        for lane in range(UNROLL):
            slot = trip * UNROLL + lane
            target = jnp.where(slot < count, pairs_ref[0, slot], clusters)
            columns = pl.ds(pl.multiple_of(target * width, width), width)
            total[:, columns] += jnp.dot(
                mixed_ref[pairs_ref[1, slot]], tiles_ref[slot], preferred_element_type=jnp.float32
            )
        return carry

    lax.fori_loop(first, last, body, 0)


def fetch(sources, targets, sems):
    copies = []
    for item, (source, target) in enumerate(zip(sources, targets)):
        copies.append(pltpu.make_async_copy(source, target, sems.at[item]))
    for copy in copies:
        copy.start()
    for copy in copies:
        copy.wait()


def first_kernel(
    pairs_hbm,
    count_hbm,
    dens_ref,
    tiles_hbm,
    mixed_ref,
    tiles_ref,
    total,
    weave,
    pairs_ref,
    count_ref,
    table_sems,
    tile_sems,
):
    fetch((pairs_hbm, count_hbm), (pairs_ref, count_ref), table_sems)
    count = count_ref[0]
    middle, last = bounds(count, 1), bounds(count, 2)
    start_tiles(tiles_hbm, tiles_ref, tile_sems, 0, last)
    weave_into(mixed_ref, dens_ref, weave)
    total[...] = jnp.zeros_like(total)

    def ready(trip):
        tile_copy(tiles_hbm, tiles_ref, tile_sems, trip).wait()

    add_tiles(0, middle, pairs_ref, count, mixed_ref, tiles_ref, total, ready)
    wait_tiles(tiles_hbm, tiles_ref, tile_sems, middle, last)


def in_place(value):
    return pltpu.with_memory_space_constraint(value, pltpu.HBM)


def near_cost(rows, tiles):
    slots, depth, width = tiles.shape
    return pl.CostEstimate(
        flops=2 * rows * depth * width * slots // 2, bytes_accessed=0, transcendentals=0
    )


def first_call(pairs, count, densities, tiles, clusters):
    rows = densities.shape[0]
    slots, depth, width = tiles.shape
    return pl.pallas_call(
        first_kernel,
        out_shape=(
            jax.ShapeDtypeStruct((clusters, rows, depth), jnp.bfloat16),
            jax.ShapeDtypeStruct(tiles.shape, tiles.dtype),
            jax.ShapeDtypeStruct((rows, (clusters + 1) * width), jnp.float32),
        ),
        in_specs=[in_hbm(), anywhere(), in_vmem(), in_hbm()],
        out_specs=(in_vmem(), in_vmem(), in_vmem()),
        scratch_shapes=[
            pltpu.VMEM((depth, depth), jnp.bfloat16),
            pltpu.SMEM(pairs.shape, pairs.dtype),
            pltpu.SMEM(count.shape, count.dtype),
            pltpu.SemaphoreType.DMA((2,)),
            pltpu.SemaphoreType.DMA((slots // UNROLL,)),
        ],
        cost_estimate=near_cost(rows, tiles),
        compiler_params=pltpu.CompilerParams(vmem_limit_bytes=16 << 20),
        name="near0",
    )(in_place(pairs), count, densities, in_place(tiles))


def second_kernel(
    pairs_hbm,
    count_hbm,
    order_hbm,
    mixed_ref,
    tiles_hbm,
    expand_hbm,
    tiles_before,
    total_before,
    tiles_ref,
    total,
    placed_ref,
    pairs_ref,
    count_ref,
    order_ref,
    table_sems,
    tile_sems,
    place_sems,
):
    clusters = mixed_ref.shape[0]
    width = tiles_ref.shape[2]
    fetch((pairs_hbm, count_hbm, order_hbm), (pairs_ref, count_ref, order_ref), table_sems)
    count = count_ref[0]
    first, middle, last = bounds(count, 1), bounds(count, 2), bounds(count, 3)
    start_tiles(tiles_hbm, tiles_ref, tile_sems, middle, last)
    copies = []
    for cluster in range(clusters):
        place = pl.multiple_of(order_ref[0, cluster] * width, width)
        copies.append(
            pltpu.make_async_copy(
                expand_hbm.at[:, :, pl.ds(cluster * width, width)],
                placed_ref.at[:, :, pl.ds(place, width)],
                place_sems.at[cluster],
            )
        )
    for copy in copies:
        copy.start()
    add_tiles(first, middle, pairs_ref, count, mixed_ref, tiles_ref, total, lambda trip: None)
    for copy in copies:
        copy.wait()
    wait_tiles(tiles_hbm, tiles_ref, tile_sems, middle, last)


def second_call(pairs, count, order, mixed, tiles, expand, fetched, total):
    clusters = mixed.shape[0]
    slots = tiles.shape[0]
    return pl.pallas_call(
        second_kernel,
        out_shape=(
            jax.ShapeDtypeStruct(fetched.shape, fetched.dtype),
            jax.ShapeDtypeStruct(total.shape, total.dtype),
            jax.ShapeDtypeStruct(expand.shape, expand.dtype),
        ),
        in_specs=[
            in_hbm(),
            anywhere(),
            in_hbm(),
            in_vmem(),
            in_hbm(),
            in_hbm(),
            in_vmem(),
            in_vmem(),
        ],
        out_specs=(in_vmem(), in_vmem(), in_vmem()),
        input_output_aliases={6: 0, 7: 1},
        scratch_shapes=[
            pltpu.SMEM(pairs.shape, pairs.dtype),
            pltpu.SMEM(count.shape, count.dtype),
            pltpu.SMEM(order.shape, order.dtype),
            pltpu.SemaphoreType.DMA((3,)),
            pltpu.SemaphoreType.DMA((slots // UNROLL,)),
            pltpu.SemaphoreType.DMA((clusters,)),
        ],
        cost_estimate=near_cost(total.shape[0], tiles),
        compiler_params=pltpu.CompilerParams(vmem_limit_bytes=16 << 20),
        name="near1",
    )(
        in_place(pairs), count, in_place(order), mixed, in_place(tiles), in_place(expand), fetched, total
    )


def third_kernel(
    pairs_hbm, count_hbm, mixed_ref, tiles_ref, before, total, pairs_ref, count_ref, table_sems
):
    fetch((pairs_hbm, count_hbm), (pairs_ref, count_ref), table_sems)
    count = count_ref[0]
    first, last = bounds(count, 2), bounds(count, 3)
    add_tiles(first, last, pairs_ref, count, mixed_ref, tiles_ref, total, lambda trip: None)


def third_call(pairs, count, mixed, fetched, total):
    return pl.pallas_call(
        third_kernel,
        out_shape=jax.ShapeDtypeStruct(total.shape, total.dtype),
        in_specs=[in_hbm(), anywhere(), in_vmem(), in_vmem(), in_vmem()],
        out_specs=in_vmem(),
        input_output_aliases={4: 0},
        scratch_shapes=[
            pltpu.SMEM(pairs.shape, pairs.dtype),
            pltpu.SMEM(count.shape, count.dtype),
            pltpu.SemaphoreType.DMA((2,)),
        ],
        cost_estimate=near_cost(total.shape[0], fetched),
        compiler_params=pltpu.CompilerParams(vmem_limit_bytes=16 << 20),
        name="near2",
    )(in_place(pairs), count, mixed, fetched, total)


def shards(
    densities, compress, level_a, level_b, expand, near_tiles, tile_pairs, tile_count, cluster_order
):
    rows, points = densities.shape
    rank = compress.shape[2]
    sections = level_a.shape[0]
    clusters = cluster_order.shape[1]
    width = points // clusters
    slots = near_tiles.shape[0]
    core = lax.axis_index("tgt").astype(jnp.int32)
    tiles = near_tiles.reshape(slots, 2 * width, width)
    pairs = tile_pairs.T
    half_rows = rows // 2

    product = jnp.dot(
        densities, compress.reshape(points, 2 * rank), preferred_element_type=jnp.float32
    )
    upper, lower = product[:half_rows], product[half_rows:]
    quarter = half_rows // 2
    first_core = core == 0
    keep, send = [], []
    for value in (upper[:, :rank] - lower[:, rank:], upper[:, rank:] + lower[:, :rank]):
        keep.append(jnp.where(first_core, value[:quarter], value[quarter:]))
        send.append(jnp.where(first_core, value[quarter:], value[:quarter]))
    keep = jnp.concatenate(keep, axis=0)
    arrived = swapped(jnp.concatenate(send, axis=0).astype(jnp.bfloat16), "tgt", 0)
    count, arrived = lax.optimization_barrier((tile_count, arrived))
    coefficients = (keep + arrived.astype(jnp.float32)).astype(jnp.bfloat16)

    def both(matrix):
        planes = matrix.transpose(0, 2, 1, 3)
        other = swapped(planes, "tgt", 0)
        joined = jnp.concatenate([planes, other], axis=3)
        return joined.reshape(sections, 2 * rank, rank)

    own_matrices, partner_matrices = both(level_a), both(level_b)
    for section in range(sections):
        partner = swapped(coefficients, "src", section)
        if section == 0:
            mixed, fetched, near = first_call(pairs, count, densities, tiles, clusters)
        elif section == 1:
            fetched, near, placed = second_call(
                pairs, count, cluster_order, mixed, tiles, expand, fetched, near
            )
        elif section == 2:
            near = third_call(pairs, count, mixed, fetched, near)
        own = jnp.dot(
            paired(coefficients), own_matrices[section], preferred_element_type=jnp.float32
        )
        updated = own + jnp.dot(
            paired(partner), partner_matrices[section], preferred_element_type=jnp.float32
        )
        updated = updated.astype(jnp.bfloat16)
        turned = jnp.concatenate([updated[:, rank // 2 :], updated[:, : rank // 2]], axis=1)
        coefficients = jnp.where(first_core, updated, turned)
    others = swapped(coefficients, "tgt", 0)
    pieces = []
    for part in range(2):
        own = coefficients[part * quarter : (part + 1) * quarter]
        other = others[part * quarter : (part + 1) * quarter]
        pieces += [jnp.where(first_core, own, other), jnp.where(first_core, other, own)]
    matrix = placed.transpose(1, 0, 2).reshape(2 * rank, points)
    far = jnp.dot(
        paired(jnp.concatenate(pieces, axis=0)), matrix, preferred_element_type=jnp.float32
    )
    return (far + near[:, :points]).astype(jnp.bfloat16)


def solution(mesh):
    placed = (
        P("grp", ("src", "tgt")),
        P(("grp", "src", "tgt"), None, None),
        P("grp", "src", None, "tgt"),
        P("grp", "src", None, "tgt"),
        P(("grp", "src"), None, "tgt"),
        P(("grp", "src", "tgt"), None, None, None),
        P(("grp", "src", "tgt"), None),
        P(("grp", "src", "tgt")),
        P(("grp", "src", "tgt"), None),
    )
    return jax.shard_map(
        shards, mesh=mesh, in_specs=placed, out_specs=P("grp", ("src", "tgt")), check_vma=False
    )
```

```python
import functools

import jax
import jax.numpy as jnp
from jax import lax
from jax.experimental import pallas as pl
from jax.experimental.pallas import tpu as pltpu
from jax.sharding import PartitionSpec as P


NEAR_SHARES = (0, 1, 4, 8)
EXPAND_CHUNKS = 4
UNROLL = 8


def in_vmem():
    return pl.BlockSpec(memory_space=pltpu.VMEM)


def in_hbm():
    return pl.BlockSpec(memory_space=pltpu.HBM)


def anywhere():
    return pl.BlockSpec(memory_space=pl.ANY)


def swapped(value, axis, bit):
    mask = 2**bit
    pairs = [(source, source ^ mask) for source in range(lax.axis_size(axis))]
    return lax.ppermute(value, axis, pairs)


def paired(block):
    half = block.shape[0] // 2
    upper, lower = block[:half], block[half:]
    return jnp.concatenate(
        [jnp.concatenate([upper, -lower], axis=1), jnp.concatenate([lower, upper], axis=1)], axis=0
    )


def prepare_weave(weave):
    width = weave.shape[0] // 2
    row_id = lax.broadcasted_iota(jnp.int32, weave.shape, 0)
    col_id = lax.broadcasted_iota(jnp.int32, weave.shape, 1)
    goal = jnp.where(row_id < width, 2 * row_id, 2 * (row_id - width) + 1)
    weave[...] = jnp.where(col_id == goal, 1.0, 0.0).astype(jnp.bfloat16)


def weave_into(mixed_ref, dens_ref, weave, first, last):
    width = dens_ref.shape[1] // mixed_ref.shape[0]
    for cluster in range(first, last):
        block = paired(dens_ref[:, cluster * width : (cluster + 1) * width])
        woven = jnp.dot(block, weave[...], preferred_element_type=jnp.float32)
        mixed_ref[cluster] = woven.astype(jnp.bfloat16)


def bounds(count, call):
    trips = (count + UNROLL - 1) // UNROLL
    return (trips * NEAR_SHARES[call]) // NEAR_SHARES[-1]


def tile_copy(tiles_hbm, tiles_ref, sems, trip):
    span = pl.ds(pl.multiple_of(trip * UNROLL, UNROLL), UNROLL)
    return pltpu.make_async_copy(tiles_hbm.at[span], tiles_ref.at[span], sems.at[trip])


def start_tiles(tiles_hbm, tiles_ref, sems, first, last):
    def body(trip, carry):
        tile_copy(tiles_hbm, tiles_ref, sems, trip).start()
        return carry

    lax.fori_loop(first, last, body, 0)


def wait_tiles(tiles_hbm, tiles_ref, sems, first, last):
    def body(trip, carry):
        tile_copy(tiles_hbm, tiles_ref, sems, trip).wait()
        return carry

    lax.fori_loop(first, last, body, 0)


def invert(order_ref, inverse_ref):
    def body(cluster, carry):
        inverse_ref[order_ref[0, cluster]] = cluster
        return carry

    lax.fori_loop(0, order_ref.shape[1], body, 0)


def add_tiles(first, last, pairs_ref, inverse_ref, count, mixed_ref, tiles_ref, total, ready):
    clusters = mixed_ref.shape[0]
    width = tiles_ref.shape[2]

    def body(trip, carry):
        ready(trip)
        for lane in range(UNROLL):
            slot = trip * UNROLL + lane
            target = jnp.where(slot < count, inverse_ref[pairs_ref[0, slot]], clusters)
            columns = pl.ds(pl.multiple_of(target * width, width), width)
            total[:, columns] += jnp.dot(
                mixed_ref[pairs_ref[1, slot]], tiles_ref[slot], preferred_element_type=jnp.float32
            )
        return carry

    lax.fori_loop(first, last, body, 0)


def fetch(sources, targets, sems):
    copies = []
    for item, (source, target) in enumerate(zip(sources, targets)):
        copies.append(pltpu.make_async_copy(source, target, sems.at[item]))
    for copy in copies:
        copy.start()

    def finish():
        for copy in copies:
            copy.wait()

    return finish


def first_kernel(
    pairs_hbm,
    count_hbm,
    order_hbm,
    dens_ref,
    tiles_hbm,
    mixed_ref,
    tiles_ref,
    total,
    weave,
    pairs_ref,
    count_ref,
    order_ref,
    inverse_ref,
    table_sems,
    tile_sems,
):
    finish = fetch(
        (pairs_hbm, count_hbm, order_hbm), (pairs_ref, count_ref, order_ref), table_sems
    )
    clusters = mixed_ref.shape[0]
    prepare_weave(weave)
    weave_into(mixed_ref, dens_ref, weave, 0, clusters // 2)
    finish()
    count = count_ref[0]
    middle, last = bounds(count, 1), bounds(count, 2)
    start_tiles(tiles_hbm, tiles_ref, tile_sems, 0, last)
    invert(order_ref, inverse_ref)
    weave_into(mixed_ref, dens_ref, weave, clusters // 2, clusters)
    total[...] = jnp.zeros_like(total)

    def ready(trip):
        tile_copy(tiles_hbm, tiles_ref, tile_sems, trip).wait()

    add_tiles(0, middle, pairs_ref, inverse_ref, count, mixed_ref, tiles_ref, total, ready)
    wait_tiles(tiles_hbm, tiles_ref, tile_sems, middle, last)


def in_place(value):
    return pltpu.with_memory_space_constraint(value, pltpu.HBM)


def near_cost(rows, tiles):
    slots, depth, width = tiles.shape
    return pl.CostEstimate(
        flops=2 * rows * depth * width * slots // 2, bytes_accessed=0, transcendentals=0
    )


def tables(*arrays):
    return [pltpu.SMEM(array.shape, array.dtype) for array in arrays]


def first_call(pairs, count, order, densities, tiles):
    rows = densities.shape[0]
    clusters = order.shape[1]
    slots, depth, width = tiles.shape
    return pl.pallas_call(
        first_kernel,
        out_shape=(
            jax.ShapeDtypeStruct((clusters, rows, depth), jnp.bfloat16),
            jax.ShapeDtypeStruct(tiles.shape, tiles.dtype),
            jax.ShapeDtypeStruct((rows, (clusters + 1) * width), jnp.float32),
        ),
        in_specs=[in_hbm(), anywhere(), in_hbm(), in_vmem(), in_hbm()],
        out_specs=(in_vmem(), in_vmem(), in_vmem()),
        scratch_shapes=[
            pltpu.VMEM((depth, depth), jnp.bfloat16),
            *tables(pairs, count, order),
            pltpu.SMEM((clusters,), jnp.int32),
            pltpu.SemaphoreType.DMA((3,)),
            pltpu.SemaphoreType.DMA((slots // UNROLL,)),
        ],
        cost_estimate=near_cost(rows, tiles),
        compiler_params=pltpu.CompilerParams(vmem_limit_bytes=16 << 20),
        name="near0",
    )(in_place(pairs), count, in_place(order), densities, in_place(tiles))


def second_kernel(
    pairs_hbm,
    count_hbm,
    order_hbm,
    mixed_ref,
    tiles_hbm,
    tiles_before,
    total_before,
    tiles_ref,
    total,
    pairs_ref,
    count_ref,
    order_ref,
    inverse_ref,
    table_sems,
    tile_sems,
):
    fetch((pairs_hbm, count_hbm, order_hbm), (pairs_ref, count_ref, order_ref), table_sems)()
    count = count_ref[0]
    first, middle, last = bounds(count, 1), bounds(count, 2), bounds(count, 3)
    start_tiles(tiles_hbm, tiles_ref, tile_sems, middle, last)
    invert(order_ref, inverse_ref)
    add_tiles(
        first, middle, pairs_ref, inverse_ref, count, mixed_ref, tiles_ref, total, lambda trip: None
    )
    wait_tiles(tiles_hbm, tiles_ref, tile_sems, middle, last)


def second_call(pairs, count, order, mixed, tiles, fetched, total):
    clusters = mixed.shape[0]
    slots = tiles.shape[0]
    return pl.pallas_call(
        second_kernel,
        out_shape=(
            jax.ShapeDtypeStruct(fetched.shape, fetched.dtype),
            jax.ShapeDtypeStruct(total.shape, total.dtype),
        ),
        in_specs=[in_hbm(), anywhere(), in_hbm(), in_vmem(), in_hbm(), in_vmem(), in_vmem()],
        out_specs=(in_vmem(), in_vmem()),
        input_output_aliases={5: 0, 6: 1},
        scratch_shapes=[
            *tables(pairs, count, order),
            pltpu.SMEM((clusters,), jnp.int32),
            pltpu.SemaphoreType.DMA((3,)),
            pltpu.SemaphoreType.DMA((slots // UNROLL,)),
        ],
        cost_estimate=near_cost(total.shape[0], tiles),
        compiler_params=pltpu.CompilerParams(vmem_limit_bytes=16 << 20),
        name="near1",
    )(in_place(pairs), count, in_place(order), mixed, in_place(tiles), fetched, total)


def third_kernel(
    pairs_hbm,
    count_hbm,
    order_hbm,
    mixed_ref,
    tiles_ref,
    before,
    total,
    pairs_ref,
    count_ref,
    order_ref,
    inverse_ref,
    table_sems,
):
    fetch((pairs_hbm, count_hbm, order_hbm), (pairs_ref, count_ref, order_ref), table_sems)()
    count = count_ref[0]
    first, last = bounds(count, 2), bounds(count, 3)
    invert(order_ref, inverse_ref)
    add_tiles(
        first, last, pairs_ref, inverse_ref, count, mixed_ref, tiles_ref, total, lambda trip: None
    )


def third_call(pairs, count, order, mixed, fetched, total):
    clusters = mixed.shape[0]
    return pl.pallas_call(
        third_kernel,
        out_shape=jax.ShapeDtypeStruct(total.shape, total.dtype),
        in_specs=[in_hbm(), anywhere(), in_hbm(), in_vmem(), in_vmem(), in_vmem()],
        out_specs=in_vmem(),
        input_output_aliases={5: 0},
        scratch_shapes=[
            *tables(pairs, count, order),
            pltpu.SMEM((clusters,), jnp.int32),
            pltpu.SemaphoreType.DMA((3,)),
        ],
        cost_estimate=near_cost(total.shape[0], fetched),
        compiler_params=pltpu.CompilerParams(vmem_limit_bytes=16 << 20),
        name="near2",
    )(in_place(pairs), count, in_place(order), mixed, fetched, total)


def expand_kernel(axis, flip, order_hbm, coeff_ref, matrix_ref, near_ref, *refs):
    out_hbm, rows_out, order_ref, table_sem, sems = refs[-5:]
    rows = near_ref.shape[0]
    quarter = rows // 4
    points = matrix_ref.shape[1]
    clusters = order_ref.shape[1]
    width = points // clusters
    finish = fetch((order_hbm,), (order_ref,), table_sem)
    core = lax.axis_index(axis)
    half = 1 - core if flip else core
    left = paired(coeff_ref[...])
    span = points // EXPAND_CHUNKS
    copies = []
    for chunk in range(EXPAND_CHUNKS):
        columns = slice(chunk * span, (chunk + 1) * span)
        far = jnp.dot(left, matrix_ref[:, columns], preferred_element_type=jnp.float32)
        for part in range(2):
            source = pl.ds(pl.multiple_of((2 * part + half) * quarter, quarter), quarter)
            inner = slice(part * quarter, (part + 1) * quarter)
            rows_out[inner, columns] = (far[inner] + near_ref[source, columns]).astype(jnp.bfloat16)
        if chunk == 0:
            finish()
        for cluster in range(chunk * clusters // EXPAND_CHUNKS, (chunk + 1) * clusters // EXPAND_CHUNKS):
            place = pl.multiple_of(order_ref[0, cluster] * width, width)
            for part in range(2):
                target = pl.ds(pl.multiple_of((2 * part + half) * quarter, quarter), quarter)
                copy = pltpu.make_async_copy(
                    rows_out.at[part * quarter : (part + 1) * quarter, cluster * width : (cluster + 1) * width],
                    out_hbm.at[target, pl.ds(place, width)],
                    sems.at[2 * cluster + part],
                )
                copy.start()
                copies.append(copy)
    for copy in copies:
        copy.wait()


def expand_call(flip, order, coefficients, matrix, near, result):
    clusters = order.shape[1]
    rows = near.shape[0]
    points = matrix.shape[1]
    operands = [in_place(order), coefficients, matrix, near]
    specs = [in_hbm(), in_vmem(), in_vmem(), in_vmem()]
    aliases = {}
    if result is not None:
        operands.append(result)
        specs.append(in_hbm())
        aliases = {4: 0}
    return pl.pallas_call(
        functools.partial(expand_kernel, "tgt", flip),
        out_shape=jax.ShapeDtypeStruct((rows, points), jnp.bfloat16),
        in_specs=specs,
        out_specs=in_hbm(),
        input_output_aliases=aliases,
        scratch_shapes=[
            pltpu.VMEM((rows // 2, points), jnp.bfloat16),
            pltpu.SMEM(order.shape, order.dtype),
            pltpu.SemaphoreType.DMA((1,)),
            pltpu.SemaphoreType.DMA((2 * clusters,)),
        ],
        cost_estimate=pl.CostEstimate(
            flops=4 * rows * matrix.shape[0] * points // 4, bytes_accessed=0, transcendentals=0
        ),
        compiler_params=pltpu.CompilerParams(vmem_limit_bytes=16 << 20),
        name="expand1" if flip else "expand0",
    )(*operands)


def shards(
    densities, compress, level_a, level_b, expand, near_tiles, tile_pairs, tile_count, cluster_order
):
    rows, points = densities.shape
    rank = compress.shape[2]
    sections = level_a.shape[0]
    clusters = cluster_order.shape[1]
    width = points // clusters
    slots = near_tiles.shape[0]
    core = lax.axis_index("tgt").astype(jnp.int32)
    tiles = near_tiles.reshape(slots, 2 * width, width)
    pairs = tile_pairs.T
    half_rows = rows // 2

    product = jnp.dot(
        densities, compress.reshape(points, 2 * rank), preferred_element_type=jnp.float32
    )
    upper, lower = product[:half_rows], product[half_rows:]
    quarter = half_rows // 2
    first_core = core == 0
    keep, send = [], []
    for value in (upper[:, :rank] - lower[:, rank:], upper[:, rank:] + lower[:, :rank]):
        keep.append(jnp.where(first_core, value[:quarter], value[quarter:]))
        send.append(jnp.where(first_core, value[quarter:], value[:quarter]))
    keep = jnp.concatenate(keep, axis=0)
    arrived = swapped(jnp.concatenate(send, axis=0).astype(jnp.bfloat16), "tgt", 0)
    count = tile_count
    coefficients = (keep + arrived.astype(jnp.float32)).astype(jnp.bfloat16)

    def both(matrix):
        planes = matrix.transpose(0, 2, 1, 3)
        other = swapped(planes, "tgt", 0)
        joined = jnp.concatenate([planes, other], axis=3)
        return joined.reshape(sections, 2 * rank, rank)

    own_matrices, partner_matrices = both(level_a), both(level_b)
    for section in range(sections):
        partner = swapped(coefficients, "src", section)
        if section == 0:
            mixed, fetched, near = first_call(pairs, count, cluster_order, densities, tiles)
        elif section == 1:
            fetched, near = second_call(pairs, count, cluster_order, mixed, tiles, fetched, near)
        elif section == 2:
            near = third_call(pairs, count, cluster_order, mixed, fetched, near)
        own = jnp.dot(
            paired(coefficients), own_matrices[section], preferred_element_type=jnp.float32
        )
        own = lax.optimization_barrier(own)
        updated = own + jnp.dot(
            paired(partner), partner_matrices[section], preferred_element_type=jnp.float32
        )
        updated = updated.astype(jnp.bfloat16)
        turned = jnp.concatenate([updated[:, rank // 2 :], updated[:, : rank // 2]], axis=1)
        coefficients = jnp.where(first_core, updated, turned)
    others = swapped(coefficients, "tgt", 0)
    matrix = expand.transpose(1, 0, 2).reshape(2 * rank, points)
    result = expand_call(False, cluster_order, coefficients, matrix, near, None)
    return expand_call(True, cluster_order, others, matrix, near, result)


def solution(mesh):
    placed = (
        P("grp", ("src", "tgt")),
        P(("grp", "src", "tgt"), None, None),
        P("grp", "src", None, "tgt"),
        P("grp", "src", None, "tgt"),
        P(("grp", "src"), None, "tgt"),
        P(("grp", "src", "tgt"), None, None, None),
        P(("grp", "src", "tgt"), None),
        P(("grp", "src", "tgt")),
        P(("grp", "src", "tgt"), None),
    )
    return jax.shard_map(
        shards, mesh=mesh, in_specs=placed, out_specs=P("grp", ("src", "tgt")), check_vma=False
    )
```

```python
import jax
import jax.numpy as jnp
from jax import lax
from jax.experimental import pallas as pl
from jax.experimental.pallas import tpu as pltpu
from jax.sharding import PartitionSpec as P


NEAR_SHARES = (0, 0, 3, 8)
FETCH_SHARES = (0, 5, 8)
EXPAND_CHUNKS = 4
UNROLL = 8


def in_vmem():
    return pl.BlockSpec(memory_space=pltpu.VMEM)


def in_hbm():
    return pl.BlockSpec(memory_space=pltpu.HBM)


def anywhere():
    return pl.BlockSpec(memory_space=pl.ANY)


def swapped(value, axis, bit):
    mask = 2**bit
    pairs = [(source, source ^ mask) for source in range(lax.axis_size(axis))]
    return lax.ppermute(value, axis, pairs)


def paired(block):
    half = block.shape[0] // 2
    upper, lower = block[:half], block[half:]
    return jnp.concatenate(
        [jnp.concatenate([upper, -lower], axis=1), jnp.concatenate([lower, upper], axis=1)], axis=0
    )


def prepare_weave(weave):
    width = weave.shape[0] // 2
    row_id = lax.broadcasted_iota(jnp.int32, weave.shape, 0)
    col_id = lax.broadcasted_iota(jnp.int32, weave.shape, 1)
    goal = jnp.where(row_id < width, 2 * row_id, 2 * (row_id - width) + 1)
    weave[...] = jnp.where(col_id == goal, 1.0, 0.0).astype(jnp.bfloat16)


def weave_into(mixed_ref, dens_ref, weave, first, last):
    width = dens_ref.shape[1] // mixed_ref.shape[0]
    for cluster in range(first, last):
        block = paired(dens_ref[:, cluster * width : (cluster + 1) * width])
        woven = jnp.dot(block, weave[...], preferred_element_type=jnp.float32)
        mixed_ref[cluster] = woven.astype(jnp.bfloat16)


def bounds(count, shares, call):
    trips = (count + UNROLL - 1) // UNROLL
    return (trips * shares[call] + shares[-1] - 1) // shares[-1]


def tile_copy(tiles_hbm, tiles_ref, sems, trip):
    span = pl.ds(pl.multiple_of(trip * UNROLL, UNROLL), UNROLL)
    return pltpu.make_async_copy(tiles_hbm.at[span], tiles_ref.at[span], sems.at[trip])


def start_tiles(tiles_hbm, tiles_ref, sems, first, last):
    def body(trip, carry):
        tile_copy(tiles_hbm, tiles_ref, sems, trip).start()
        return carry

    lax.fori_loop(first, last, body, 0)


def wait_tiles(tiles_hbm, tiles_ref, sems, first, last):
    def body(trip, carry):
        tile_copy(tiles_hbm, tiles_ref, sems, trip).wait()
        return carry

    lax.fori_loop(first, last, body, 0)


def invert(order_ref, inverse_ref):
    def body(cluster, carry):
        inverse_ref[order_ref[0, cluster]] = cluster
        return carry

    lax.fori_loop(0, order_ref.shape[1], body, 0)


def add_tiles(first, last, pairs_ref, inverse_ref, count, mixed_ref, tiles_ref, total):
    clusters = mixed_ref.shape[0]
    width = tiles_ref.shape[2]

    def body(trip, carry):
        for lane in range(UNROLL):
            slot = trip * UNROLL + lane
            target = jnp.where(slot < count, inverse_ref[pairs_ref[0, slot]], clusters)
            columns = pl.ds(pl.multiple_of(target * width, width), width)
            total[:, columns] += jnp.dot(
                mixed_ref[pairs_ref[1, slot]], tiles_ref[slot], preferred_element_type=jnp.float32
            )
        return carry

    lax.fori_loop(first, last, body, 0)


def fetch(sources, targets, sems):
    copies = []
    for item, (source, target) in enumerate(zip(sources, targets)):
        copies.append(pltpu.make_async_copy(source, target, sems.at[item]))
    for copy in copies:
        copy.start()

    def finish():
        for copy in copies:
            copy.wait()

    return finish


def first_kernel(
    count_hbm, dens_ref, tiles_hbm, mixed_ref, tiles_ref, total, weave, count_ref, table_sem, tile_sems
):
    finish = fetch((count_hbm,), (count_ref,), table_sem)
    clusters = mixed_ref.shape[0]
    prepare_weave(weave)
    weave_into(mixed_ref, dens_ref, weave, 0, clusters // 2)
    finish()
    count = count_ref[0]
    last = bounds(count, FETCH_SHARES, 1)
    start_tiles(tiles_hbm, tiles_ref, tile_sems, 0, last)
    weave_into(mixed_ref, dens_ref, weave, clusters // 2, clusters)
    total[...] = jnp.zeros_like(total)

    wait_tiles(tiles_hbm, tiles_ref, tile_sems, 0, last)


def in_place(value):
    return pltpu.with_memory_space_constraint(value, pltpu.HBM)


def near_cost(rows, tiles):
    slots, depth, width = tiles.shape
    return pl.CostEstimate(
        flops=2 * rows * depth * width * slots // 2, bytes_accessed=0, transcendentals=0
    )


def tables(*arrays):
    return [pltpu.SMEM(array.shape, array.dtype) for array in arrays]


def first_call(count, densities, tiles, clusters):
    rows = densities.shape[0]
    slots, depth, width = tiles.shape
    return pl.pallas_call(
        first_kernel,
        out_shape=(
            jax.ShapeDtypeStruct((clusters, rows, depth), jnp.bfloat16),
            jax.ShapeDtypeStruct(tiles.shape, tiles.dtype),
            jax.ShapeDtypeStruct((rows, (clusters + 1) * width), jnp.float32),
        ),
        in_specs=[anywhere(), in_vmem(), in_hbm()],
        out_specs=(in_vmem(), in_vmem(), in_vmem()),
        scratch_shapes=[
            pltpu.VMEM((depth, depth), jnp.bfloat16),
            *tables(count),
            pltpu.SemaphoreType.DMA((1,)),
            pltpu.SemaphoreType.DMA((slots // UNROLL,)),
        ],
        cost_estimate=near_cost(rows, tiles),
        compiler_params=pltpu.CompilerParams(vmem_limit_bytes=16 << 20),
        name="near0",
    )(count, densities, in_place(tiles))


def second_kernel(
    pairs_hbm,
    count_hbm,
    order_hbm,
    mixed_ref,
    tiles_hbm,
    tiles_before,
    total_before,
    tiles_ref,
    total,
    pairs_ref,
    count_ref,
    order_ref,
    inverse_ref,
    table_sems,
    tile_sems,
):
    fetch((pairs_hbm, count_hbm, order_hbm), (pairs_ref, count_ref, order_ref), table_sems)()
    count = count_ref[0]
    first, last = bounds(count, FETCH_SHARES, 1), bounds(count, FETCH_SHARES, 2)
    start_tiles(tiles_hbm, tiles_ref, tile_sems, first, last)
    invert(order_ref, inverse_ref)
    end = bounds(count, NEAR_SHARES, 2)
    add_tiles(0, end, pairs_ref, inverse_ref, count, mixed_ref, tiles_ref, total)
    wait_tiles(tiles_hbm, tiles_ref, tile_sems, first, last)


def second_call(pairs, count, order, mixed, tiles, fetched, total):
    clusters = mixed.shape[0]
    slots = tiles.shape[0]
    return pl.pallas_call(
        second_kernel,
        out_shape=(
            jax.ShapeDtypeStruct(fetched.shape, fetched.dtype),
            jax.ShapeDtypeStruct(total.shape, total.dtype),
        ),
        in_specs=[in_hbm(), anywhere(), in_hbm(), in_vmem(), in_hbm(), in_vmem(), in_vmem()],
        out_specs=(in_vmem(), in_vmem()),
        input_output_aliases={5: 0, 6: 1},
        scratch_shapes=[
            *tables(pairs, count, order),
            pltpu.SMEM((clusters,), jnp.int32),
            pltpu.SemaphoreType.DMA((3,)),
            pltpu.SemaphoreType.DMA((slots // UNROLL,)),
        ],
        cost_estimate=near_cost(total.shape[0], tiles),
        compiler_params=pltpu.CompilerParams(vmem_limit_bytes=16 << 20),
        name="near1",
    )(in_place(pairs), count, in_place(order), mixed, in_place(tiles), fetched, total)


def third_kernel(
    pairs_hbm,
    count_hbm,
    order_hbm,
    mixed_ref,
    tiles_ref,
    before,
    total,
    pairs_ref,
    count_ref,
    order_ref,
    inverse_ref,
    table_sems,
):
    fetch((pairs_hbm, count_hbm, order_hbm), (pairs_ref, count_ref, order_ref), table_sems)()
    count = count_ref[0]
    invert(order_ref, inverse_ref)
    first, last = bounds(count, NEAR_SHARES, 2), bounds(count, NEAR_SHARES, 3)
    add_tiles(first, last, pairs_ref, inverse_ref, count, mixed_ref, tiles_ref, total)


def third_call(pairs, count, order, mixed, fetched, total):
    clusters = mixed.shape[0]
    return pl.pallas_call(
        third_kernel,
        out_shape=jax.ShapeDtypeStruct(total.shape, total.dtype),
        in_specs=[in_hbm(), anywhere(), in_hbm(), in_vmem(), in_vmem(), in_vmem()],
        out_specs=in_vmem(),
        input_output_aliases={5: 0},
        scratch_shapes=[
            *tables(pairs, count, order),
            pltpu.SMEM((clusters,), jnp.int32),
            pltpu.SemaphoreType.DMA((3,)),
        ],
        cost_estimate=near_cost(total.shape[0], fetched),
        compiler_params=pltpu.CompilerParams(vmem_limit_bytes=16 << 20),
        name="near2",
    )(in_place(pairs), count, in_place(order), mixed, fetched, total)


def far_rows(half, coeff_ref, matrix_ref, near_ref, rows_ref, columns):
    quarter = near_ref.shape[0] // 4
    far = jnp.dot(
        paired(coeff_ref[...]), matrix_ref[:, columns], preferred_element_type=jnp.float32
    )
    for part in range(2):
        source = pl.ds(pl.multiple_of((2 * part + half) * quarter, quarter), quarter)
        inner = slice(part * quarter, (part + 1) * quarter)
        rows_ref[inner, columns] = (far[inner] + near_ref[source, columns]).astype(jnp.bfloat16)


def own_kernel(coeff_ref, matrix_ref, near_ref, rows_ref):
    span = matrix_ref.shape[1] // EXPAND_CHUNKS
    for chunk in range(EXPAND_CHUNKS):
        columns = slice(chunk * span, (chunk + 1) * span)
        far_rows(lax.axis_index("tgt"), coeff_ref, matrix_ref, near_ref, rows_ref, columns)


def expand_cost(coefficients, matrix):
    return pl.CostEstimate(
        flops=4 * coefficients.size * matrix.shape[1], bytes_accessed=0, transcendentals=0
    )


def own_call(coefficients, matrix, near):
    return pl.pallas_call(
        own_kernel,
        out_shape=jax.ShapeDtypeStruct((coefficients.shape[0], matrix.shape[1]), jnp.bfloat16),
        in_specs=[in_vmem(), in_vmem(), in_vmem()],
        out_specs=in_vmem(),
        cost_estimate=expand_cost(coefficients, matrix),
        compiler_params=pltpu.CompilerParams(vmem_limit_bytes=16 << 20),
        name="expand0",
    )(coefficients, matrix, near)


def last_kernel(order_ref, early_ref, coeff_ref, matrix_ref, near_ref, out_hbm, rows_ref, sems):
    quarter = near_ref.shape[0] // 4
    points = matrix_ref.shape[1]
    clusters = order_ref.shape[1]
    width = points // clusters
    core = lax.axis_index("tgt")
    order = order_ref[...]
    copies = []

    def send(buffer, half, cluster, sem):
        place = pl.multiple_of(order[0, cluster] * width, width)
        for part in range(2):
            target = pl.ds(pl.multiple_of((2 * part + half) * quarter, quarter), quarter)
            copy = pltpu.make_async_copy(
                buffer.at[
                    part * quarter : (part + 1) * quarter, cluster * width : (cluster + 1) * width
                ],
                out_hbm.at[target, pl.ds(place, width)],
                sems.at[sem + 2 * cluster + part],
            )
            copy.start()
            copies.append(copy)

    for cluster in range(clusters):
        send(early_ref, core, cluster, 0)
    span = points // EXPAND_CHUNKS
    for chunk in range(EXPAND_CHUNKS):
        columns = slice(chunk * span, (chunk + 1) * span)
        far_rows(1 - core, coeff_ref, matrix_ref, near_ref, rows_ref, columns)
        for cluster in range(
            chunk * clusters // EXPAND_CHUNKS, (chunk + 1) * clusters // EXPAND_CHUNKS
        ):
            send(rows_ref, 1 - core, cluster, 2 * clusters)
    for copy in copies:
        copy.wait()


def last_call(order, early, coefficients, matrix, near):
    rows = near.shape[0]
    points = matrix.shape[1]
    return pl.pallas_call(
        last_kernel,
        out_shape=jax.ShapeDtypeStruct((rows, points), jnp.bfloat16),
        in_specs=[in_vmem()] * 5,
        out_specs=in_hbm(),
        scratch_shapes=[
            pltpu.VMEM((rows // 2, points), jnp.bfloat16),
            pltpu.SemaphoreType.DMA((4 * order.shape[1],)),
        ],
        cost_estimate=expand_cost(coefficients, matrix),
        compiler_params=pltpu.CompilerParams(vmem_limit_bytes=16 << 20),
        name="expand1",
    )(order, early, coefficients, matrix, near)


def shards(
    densities, compress, level_a, level_b, expand, near_tiles, tile_pairs, tile_count, cluster_order
):
    rows, points = densities.shape
    rank = compress.shape[2]
    sections = level_a.shape[0]
    clusters = cluster_order.shape[1]
    width = points // clusters
    slots = near_tiles.shape[0]
    core = lax.axis_index("tgt").astype(jnp.int32)
    tiles = near_tiles.reshape(slots, 2 * width, width)
    pairs = tile_pairs.T
    half_rows = rows // 2

    product = jnp.dot(
        densities, compress.reshape(points, 2 * rank), preferred_element_type=jnp.float32
    )
    upper, lower = product[:half_rows], product[half_rows:]
    quarter = half_rows // 2
    first_core = core == 0
    keep, send = [], []
    for value in (upper[:, :rank] - lower[:, rank:], upper[:, rank:] + lower[:, :rank]):
        keep.append(jnp.where(first_core, value[:quarter], value[quarter:]))
        send.append(jnp.where(first_core, value[quarter:], value[:quarter]))
    keep = jnp.concatenate(keep, axis=0)
    arrived = swapped(jnp.concatenate(send, axis=0).astype(jnp.bfloat16), "tgt", 0)
    count = tile_count
    coefficients = (keep + arrived.astype(jnp.float32)).astype(jnp.bfloat16)

    def both(matrix):
        planes = matrix.transpose(0, 2, 1, 3)
        other = swapped(planes, "tgt", 0)
        joined = jnp.concatenate([planes, other], axis=3)
        return joined.reshape(sections, 2 * rank, rank)

    own_matrices, partner_matrices = both(level_a), both(level_b)
    for section in range(sections):
        partner = swapped(coefficients, "src", section)
        if section == 0:
            mixed, fetched, near = first_call(count, densities, tiles, clusters)
        elif section == 1:
            fetched, near = second_call(pairs, count, cluster_order, mixed, tiles, fetched, near)
        elif section == 2:
            near = third_call(pairs, count, cluster_order, mixed, fetched, near)
        own = jnp.dot(
            paired(coefficients), own_matrices[section], preferred_element_type=jnp.float32
        )
        own = lax.optimization_barrier(own)
        updated = own + jnp.dot(
            paired(partner), partner_matrices[section], preferred_element_type=jnp.float32
        )
        updated = updated.astype(jnp.bfloat16)
        turned = jnp.concatenate([updated[:, rank // 2 :], updated[:, : rank // 2]], axis=1)
        coefficients = jnp.where(first_core, updated, turned)
    others = swapped(coefficients, "tgt", 0)
    matrix = expand.transpose(1, 0, 2).reshape(2 * rank, points)
    early = own_call(coefficients, matrix, near)
    return last_call(cluster_order, early, others, matrix, near)


def solution(mesh):
    placed = (
        P("grp", ("src", "tgt")),
        P(("grp", "src", "tgt"), None, None),
        P("grp", "src", None, "tgt"),
        P("grp", "src", None, "tgt"),
        P(("grp", "src"), None, "tgt"),
        P(("grp", "src", "tgt"), None, None, None),
        P(("grp", "src", "tgt"), None),
        P(("grp", "src", "tgt")),
        P(("grp", "src", "tgt"), None),
    )
    return jax.shard_map(
        shards, mesh=mesh, in_specs=placed, out_specs=P("grp", ("src", "tgt")), check_vma=False
    )
```

```python
import functools

import jax
import jax.numpy as jnp
from jax import lax
from jax.experimental import pallas as pl
from jax.experimental.pallas import tpu as pltpu
from jax.sharding import PartitionSpec as P


EXPAND_CHUNKS = 4
UNROLL = 16


def in_vmem():
    return pl.BlockSpec(memory_space=pltpu.VMEM)


def in_smem():
    return pl.BlockSpec(memory_space=pltpu.SMEM)


def in_hbm():
    return pl.BlockSpec(memory_space=pltpu.HBM)


def swapped(value, axis, bit):
    mask = 2**bit
    pairs = [(source, source ^ mask) for source in range(lax.axis_size(axis))]
    return lax.ppermute(value, axis, pairs)


def paired(block):
    half = block.shape[0] // 2
    upper, lower = block[:half], block[half:]
    return jnp.concatenate(
        [jnp.concatenate([upper, -lower], axis=1), jnp.concatenate([lower, upper], axis=1)], axis=0
    )


def first_kernel(dens_ref, mixed_ref, total, weave):
    clusters = mixed_ref.shape[0]
    width = dens_ref.shape[1] // clusters
    row_id = lax.broadcasted_iota(jnp.int32, weave.shape, 0)
    col_id = lax.broadcasted_iota(jnp.int32, weave.shape, 1)
    goal = jnp.where(row_id < width, 2 * row_id, 2 * (row_id - width) + 1)
    weave[...] = jnp.where(col_id == goal, 1.0, 0.0).astype(jnp.bfloat16)
    for cluster in range(clusters):
        block = paired(dens_ref[:, cluster * width : (cluster + 1) * width])
        woven = jnp.dot(block, weave[...], preferred_element_type=jnp.float32)
        mixed_ref[cluster] = woven.astype(jnp.bfloat16)
    total[...] = jnp.zeros_like(total)


def tiles_kernel(first, last, table_ref, count_ref, mixed_ref, tiles_ref, before, total):
    clusters = mixed_ref.shape[0]
    width = tiles_ref.shape[2]
    count = count_ref[0]
    for start in range(first, last, UNROLL):

        @pl.when(start < count)
        def _():
            table = table_ref[...]
            for slot in range(start, min(start + UNROLL, last)):
                target = jnp.where(slot < count, table[0, slot], clusters)
                columns = pl.ds(pl.multiple_of(target * width, width), width)
                total[:, columns] += jnp.dot(
                    mixed_ref[table[1, slot]], tiles_ref[slot], preferred_element_type=jnp.float32
                )


def first_call(densities, clusters):
    rows, points = densities.shape
    width = points // clusters
    return pl.pallas_call(
        first_kernel,
        out_shape=(
            jax.ShapeDtypeStruct((clusters, rows, 2 * width), jnp.bfloat16),
            jax.ShapeDtypeStruct((rows, points + width), jnp.float32),
        ),
        in_specs=[in_vmem()],
        out_specs=(in_vmem(), in_vmem()),
        scratch_shapes=[pltpu.VMEM((2 * width, 2 * width), jnp.bfloat16)],
        cost_estimate=pl.CostEstimate(
            flops=4 * rows * points * width, bytes_accessed=0, transcendentals=0
        ),
        compiler_params=pltpu.CompilerParams(vmem_limit_bytes=16 << 20),
        name="weave",
    )(densities)


def tiles_call(first, last, table, count, mixed, tiles, total):
    depth, width = tiles.shape[1:]
    return pl.pallas_call(
        functools.partial(tiles_kernel, first, last),
        out_shape=jax.ShapeDtypeStruct(total.shape, total.dtype),
        in_specs=[in_vmem(), in_smem(), in_vmem(), in_vmem(), in_vmem()],
        out_specs=in_vmem(),
        input_output_aliases={4: 0},
        cost_estimate=pl.CostEstimate(
            flops=2 * total.shape[0] * depth * width * (last - first),
            bytes_accessed=0,
            transcendentals=0,
        ),
        compiler_params=pltpu.CompilerParams(vmem_limit_bytes=16 << 20),
        name="tiles",
    )(table, count, mixed, tiles, total)


def far_rows(half, coeff_ref, matrix_ref, near_ref, rows_ref, columns):
    quarter = near_ref.shape[0] // 4
    far = jnp.dot(
        paired(coeff_ref[...]), matrix_ref[:, columns], preferred_element_type=jnp.float32
    )
    for part in range(2):
        source = pl.ds(pl.multiple_of((2 * part + half) * quarter, quarter), quarter)
        inner = slice(part * quarter, (part + 1) * quarter)
        rows_ref[inner, columns] = (far[inner] + near_ref[source, columns]).astype(jnp.bfloat16)


def own_kernel(coeff_ref, matrix_ref, near_ref, rows_ref):
    span = matrix_ref.shape[1] // EXPAND_CHUNKS
    for chunk in range(EXPAND_CHUNKS):
        columns = slice(chunk * span, (chunk + 1) * span)
        far_rows(lax.axis_index("tgt"), coeff_ref, matrix_ref, near_ref, rows_ref, columns)


def expand_cost(coefficients, matrix):
    return pl.CostEstimate(
        flops=4 * coefficients.size * matrix.shape[1], bytes_accessed=0, transcendentals=0
    )


def own_call(coefficients, matrix, near):
    return pl.pallas_call(
        own_kernel,
        out_shape=jax.ShapeDtypeStruct((coefficients.shape[0], matrix.shape[1]), jnp.bfloat16),
        in_specs=[in_vmem(), in_vmem(), in_vmem()],
        out_specs=in_vmem(),
        cost_estimate=expand_cost(coefficients, matrix),
        compiler_params=pltpu.CompilerParams(vmem_limit_bytes=16 << 20),
        name="expand0",
    )(coefficients, matrix, near)


def last_kernel(order_ref, early_ref, coeff_ref, matrix_ref, near_ref, out_hbm, rows_ref, sems):
    quarter = near_ref.shape[0] // 4
    points = matrix_ref.shape[1]
    clusters = order_ref.shape[1]
    width = points // clusters
    core = lax.axis_index("tgt")
    order = order_ref[...]

    def send(buffer, half, cluster, sem):
        place = pl.multiple_of(order[0, cluster] * width, width)
        for part in range(2):
            target = pl.ds(pl.multiple_of((2 * part + half) * quarter, quarter), quarter)
            pltpu.make_async_copy(
                buffer.at[
                    part * quarter : (part + 1) * quarter, cluster * width : (cluster + 1) * width
                ],
                out_hbm.at[target, pl.ds(place, width)],
                sem,
            ).start()

    for cluster in range(clusters):
        send(early_ref, core, cluster, sems.at[0])
    span = points // EXPAND_CHUNKS
    for chunk in range(EXPAND_CHUNKS):
        columns = slice(chunk * span, (chunk + 1) * span)
        far_rows(1 - core, coeff_ref, matrix_ref, near_ref, rows_ref, columns)
        for cluster in range(
            chunk * clusters // EXPAND_CHUNKS, (chunk + 1) * clusters // EXPAND_CHUNKS
        ):
            send(rows_ref, 1 - core, cluster, sems.at[1])
    whole = out_hbm.at[0 : 2 * quarter, :]
    pltpu.make_async_copy(early_ref, whole, sems.at[0]).wait()
    pltpu.make_async_copy(rows_ref, whole, sems.at[1]).wait()


def last_call(order, early, coefficients, matrix, near):
    rows = near.shape[0]
    points = matrix.shape[1]
    return pl.pallas_call(
        last_kernel,
        out_shape=jax.ShapeDtypeStruct((rows, points), jnp.bfloat16),
        in_specs=[in_vmem()] * 5,
        out_specs=in_hbm(),
        scratch_shapes=[
            pltpu.VMEM((rows // 2, points), jnp.bfloat16),
            pltpu.SemaphoreType.DMA((2,)),
        ],
        cost_estimate=expand_cost(coefficients, matrix),
        compiler_params=pltpu.CompilerParams(vmem_limit_bytes=16 << 20),
        name="expand1",
    )(order, early, coefficients, matrix, near)


def shards(
    densities, compress, level_a, level_b, expand, near_tiles, tile_pairs, tile_count, cluster_order
):
    rows, points = densities.shape
    rank = compress.shape[2]
    sections = level_a.shape[0]
    clusters = cluster_order.shape[1]
    width = points // clusters
    slots = near_tiles.shape[0]
    core = lax.axis_index("tgt").astype(jnp.int32)
    tiles = near_tiles.reshape(slots, 2 * width, width)
    ids = jnp.arange(clusters, dtype=jnp.int32)
    found = cluster_order[0][None, :] == tile_pairs[:, 0][:, None]
    places = jnp.sum(jnp.where(found, ids[None, :], 0), axis=1)
    table = jnp.stack([places, tile_pairs[:, 1]])
    cut = slots // UNROLL // 2 * UNROLL
    half_rows = rows // 2

    product = jnp.dot(
        densities, compress.reshape(points, 2 * rank), preferred_element_type=jnp.float32
    )
    upper, lower = product[:half_rows], product[half_rows:]
    quarter = half_rows // 2
    first_core = core == 0
    keep, send = [], []
    for value in (upper[:, :rank] - lower[:, rank:], upper[:, rank:] + lower[:, :rank]):
        keep.append(jnp.where(first_core, value[:quarter], value[quarter:]))
        send.append(jnp.where(first_core, value[quarter:], value[:quarter]))
    keep = jnp.concatenate(keep, axis=0)
    arrived = swapped(jnp.concatenate(send, axis=0).astype(jnp.bfloat16), "tgt", 0)
    coefficients = (keep + arrived.astype(jnp.float32)).astype(jnp.bfloat16)

    def both(matrix):
        planes = matrix.transpose(0, 2, 1, 3)
        other = swapped(planes, "tgt", 0)
        joined = jnp.concatenate([planes, other], axis=3)
        return joined.reshape(sections, 2 * rank, rank)

    own_matrices, partner_matrices = both(level_a), both(level_b)
    for section in range(sections):
        partner = swapped(coefficients, "src", section)
        if section == 0:
            mixed, near = first_call(densities, clusters)
        elif section == 1:
            near = tiles_call(0, cut, table, tile_count, mixed, tiles, near)
        elif section == 2:
            near = tiles_call(cut, slots, table, tile_count, mixed, tiles, near)
        own = jnp.dot(
            paired(coefficients), own_matrices[section], preferred_element_type=jnp.float32
        )
        own = lax.optimization_barrier(own)
        updated = own + jnp.dot(
            paired(partner), partner_matrices[section], preferred_element_type=jnp.float32
        )
        updated = updated.astype(jnp.bfloat16)
        turned = jnp.concatenate([updated[:, rank // 2 :], updated[:, : rank // 2]], axis=1)
        coefficients = jnp.where(first_core, updated, turned)
    others = swapped(coefficients, "tgt", 0)
    matrix = expand.transpose(1, 0, 2).reshape(2 * rank, points)
    early = own_call(coefficients, matrix, near)
    return last_call(cluster_order, early, others, matrix, near)


def solution(mesh):
    placed = (
        P("grp", ("src", "tgt")),
        P(("grp", "src", "tgt"), None, None),
        P("grp", "src", None, "tgt"),
        P("grp", "src", None, "tgt"),
        P(("grp", "src"), None, "tgt"),
        P(("grp", "src", "tgt"), None, None, None),
        P(("grp", "src", "tgt"), None),
        P(("grp", "src", "tgt")),
        P(("grp", "src", "tgt"), None),
    )
    return jax.shard_map(
        shards, mesh=mesh, in_specs=placed, out_specs=P("grp", ("src", "tgt")), check_vma=False
    )
```

```python
import functools

import jax
import jax.numpy as jnp
from jax import lax
from jax.experimental import pallas as pl
from jax.experimental.pallas import tpu as pltpu
from jax.sharding import PartitionSpec as P


EXPAND_CHUNKS = 4
UNROLL = 16


def in_vmem():
    return pl.BlockSpec(memory_space=pltpu.VMEM)


def in_smem():
    return pl.BlockSpec(memory_space=pltpu.SMEM)


def in_hbm():
    return pl.BlockSpec(memory_space=pltpu.HBM)


def swapped(value, axis, bit):
    mask = 2**bit
    pairs = [(source, source ^ mask) for source in range(lax.axis_size(axis))]
    return lax.ppermute(value, axis, pairs)


def paired(block):
    half = block.shape[0] // 2
    upper, lower = block[:half], block[half:]
    return jnp.concatenate(
        [jnp.concatenate([upper, -lower], axis=1), jnp.concatenate([lower, upper], axis=1)], axis=0
    )


def first_kernel(dens_ref, mixed_ref, total, weave):
    clusters = mixed_ref.shape[0]
    width = dens_ref.shape[1] // clusters
    row_id = lax.broadcasted_iota(jnp.int32, weave.shape, 0)
    col_id = lax.broadcasted_iota(jnp.int32, weave.shape, 1)
    goal = jnp.where(row_id < width, 2 * row_id, 2 * (row_id - width) + 1)
    weave[...] = jnp.where(col_id == goal, 1.0, 0.0).astype(jnp.bfloat16)
    for cluster in range(clusters):
        block = paired(dens_ref[:, cluster * width : (cluster + 1) * width])
        woven = jnp.dot(block, weave[...], preferred_element_type=jnp.float32)
        mixed_ref[cluster] = woven.astype(jnp.bfloat16)
    total[...] = jnp.zeros_like(total)


def tiles_kernel(first, last, table_ref, count_ref, mixed_ref, tiles_ref, before, total):
    clusters = mixed_ref.shape[0]
    width = tiles_ref.shape[2]
    count = count_ref[0]
    for start in range(first, last, UNROLL):

        @pl.when(start < count)
        def _():
            table = table_ref[...]
            for slot in range(start, min(start + UNROLL, last)):
                target = jnp.where(slot < count, table[0, slot], clusters)
                columns = pl.ds(pl.multiple_of(target * width, width), width)
                total[:, columns] += jnp.dot(
                    mixed_ref[table[1, slot]], tiles_ref[slot], preferred_element_type=jnp.float32
                )


def first_call(densities, clusters):
    rows, points = densities.shape
    width = points // clusters
    return pl.pallas_call(
        first_kernel,
        out_shape=(
            jax.ShapeDtypeStruct((clusters, rows, 2 * width), jnp.bfloat16),
            jax.ShapeDtypeStruct((rows, points + width), jnp.float32),
        ),
        in_specs=[in_vmem()],
        out_specs=(in_vmem(), in_vmem()),
        scratch_shapes=[pltpu.VMEM((2 * width, 2 * width), jnp.bfloat16)],
        cost_estimate=pl.CostEstimate(
            flops=4 * rows * points * width, bytes_accessed=0, transcendentals=0
        ),
        compiler_params=pltpu.CompilerParams(vmem_limit_bytes=16 << 20),
        name="weave",
    )(densities)


def tiles_call(first, last, table, count, mixed, tiles, total):
    depth, width = tiles.shape[1:]
    return pl.pallas_call(
        functools.partial(tiles_kernel, first, last),
        out_shape=jax.ShapeDtypeStruct(total.shape, total.dtype),
        in_specs=[in_vmem(), in_smem(), in_vmem(), in_vmem(), in_vmem()],
        out_specs=in_vmem(),
        input_output_aliases={4: 0},
        cost_estimate=pl.CostEstimate(
            flops=2 * total.shape[0] * depth * width * (last - first),
            bytes_accessed=0,
            transcendentals=0,
        ),
        compiler_params=pltpu.CompilerParams(vmem_limit_bytes=16 << 20),
        name="tiles",
    )(table, count, mixed, tiles, total)


def far_rows(half, coeff_ref, matrix_ref, near_ref, rows_ref, columns):
    quarter = near_ref.shape[0] // 4
    far = jnp.dot(
        paired(coeff_ref[...]), matrix_ref[:, columns], preferred_element_type=jnp.float32
    )
    for part in range(2):
        source = pl.ds(pl.multiple_of((2 * part + half) * quarter, quarter), quarter)
        inner = slice(part * quarter, (part + 1) * quarter)
        rows_ref[inner, columns] = (far[inner] + near_ref[source, columns]).astype(jnp.bfloat16)


def expand_kernel(flip, order_ref, coeff_ref, matrix_ref, near_ref, *refs):
    out_hbm, rows_ref, sem = refs[-3:]
    quarter = near_ref.shape[0] // 4
    points = matrix_ref.shape[1]
    clusters = order_ref.shape[1]
    width = points // clusters
    core = lax.axis_index("tgt")
    half = 1 - core if flip else core
    order = order_ref[...]
    span = points // EXPAND_CHUNKS
    for chunk in range(EXPAND_CHUNKS):
        columns = slice(chunk * span, (chunk + 1) * span)
        far_rows(half, coeff_ref, matrix_ref, near_ref, rows_ref, columns)
        for cluster in range(
            chunk * clusters // EXPAND_CHUNKS, (chunk + 1) * clusters // EXPAND_CHUNKS
        ):
            place = pl.multiple_of(order[0, cluster] * width, width)
            source = slice(cluster * width, (cluster + 1) * width)
            for part in range(2):
                target = pl.ds(pl.multiple_of((2 * part + half) * quarter, quarter), quarter)
                pltpu.make_async_copy(
                    rows_ref.at[part * quarter : (part + 1) * quarter, source],
                    out_hbm.at[target, pl.ds(place, width)],
                    sem.at[0],
                ).start()
    pltpu.make_async_copy(rows_ref, out_hbm.at[0 : 2 * quarter, :], sem.at[0]).wait()


def expand_call(flip, order, coefficients, matrix, near, result):
    rows = near.shape[0]
    points = matrix.shape[1]
    operands = [order, coefficients, matrix, near]
    specs = [in_vmem()] * 4
    aliases = {}
    if result is not None:
        operands.append(result)
        specs.append(in_hbm())
        aliases = {4: 0}
    return pl.pallas_call(
        functools.partial(expand_kernel, flip),
        out_shape=jax.ShapeDtypeStruct((rows, points), jnp.bfloat16),
        in_specs=specs,
        out_specs=in_hbm(),
        input_output_aliases=aliases,
        scratch_shapes=[
            pltpu.VMEM((rows // 2, points), jnp.bfloat16),
            pltpu.SemaphoreType.DMA((1,)),
        ],
        cost_estimate=pl.CostEstimate(
            flops=4 * coefficients.size * points, bytes_accessed=0, transcendentals=0
        ),
        compiler_params=pltpu.CompilerParams(vmem_limit_bytes=16 << 20),
        name="expand1" if flip else "expand0",
    )(*operands)


def shards(
    densities, compress, level_a, level_b, expand, near_tiles, tile_pairs, tile_count, cluster_order
):
    rows, points = densities.shape
    rank = compress.shape[2]
    sections = level_a.shape[0]
    clusters = cluster_order.shape[1]
    width = points // clusters
    slots = near_tiles.shape[0]
    core = lax.axis_index("tgt").astype(jnp.int32)
    tiles = near_tiles.reshape(slots, 2 * width, width)
    ids = jnp.arange(clusters, dtype=jnp.int32)
    found = cluster_order[0][None, :] == tile_pairs[:, 0][:, None]
    places = jnp.sum(jnp.where(found, ids[None, :], 0), axis=1)
    table = jnp.stack([places, tile_pairs[:, 1]])
    count = jnp.minimum(tile_count, slots)
    cut = slots * 3 // 5
    half_rows = rows // 2

    product = jnp.dot(
        densities, compress.reshape(points, 2 * rank), preferred_element_type=jnp.float32
    )
    upper, lower = product[:half_rows], product[half_rows:]
    quarter = half_rows // 2
    first_core = core == 0
    keep, send = [], []
    for value in (upper[:, :rank] - lower[:, rank:], upper[:, rank:] + lower[:, :rank]):
        keep.append(jnp.where(first_core, value[:quarter], value[quarter:]))
        send.append(jnp.where(first_core, value[quarter:], value[:quarter]))
    keep = jnp.concatenate(keep, axis=0)
    arrived = swapped(jnp.concatenate(send, axis=0).astype(jnp.bfloat16), "tgt", 0)
    coefficients = (keep + arrived.astype(jnp.float32)).astype(jnp.bfloat16)

    def both(matrix):
        planes = matrix.transpose(0, 2, 1, 3)
        other = swapped(planes, "tgt", 0)
        joined = jnp.concatenate([planes, other], axis=3)
        return joined.reshape(sections, 2 * rank, rank)

    own_matrices, partner_matrices = both(level_a), both(level_b)
    for section in range(sections):
        partner = swapped(coefficients, "src", section)
        if section == 0:
            mixed, near = first_call(densities, clusters)
        elif section == 1:
            near = tiles_call(0, cut, table, count, mixed, tiles, near)
        elif section == 2:
            near = tiles_call(cut, slots, table, count, mixed, tiles, near)
        own = jnp.dot(
            paired(coefficients), own_matrices[section], preferred_element_type=jnp.float32
        )
        own = lax.optimization_barrier(own)
        updated = own + jnp.dot(
            paired(partner), partner_matrices[section], preferred_element_type=jnp.float32
        )
        updated = updated.astype(jnp.bfloat16)
        turned = jnp.concatenate([updated[:, rank // 2 :], updated[:, : rank // 2]], axis=1)
        coefficients = jnp.where(first_core, updated, turned)
    others = swapped(coefficients, "tgt", 0)
    matrix = expand.transpose(1, 0, 2).reshape(2 * rank, points)
    result = expand_call(False, cluster_order, coefficients, matrix, near, None)
    return expand_call(True, cluster_order, others, matrix, near, result)


def solution(mesh):
    placed = (
        P("grp", ("src", "tgt")),
        P(("grp", "src", "tgt"), None, None),
        P("grp", "src", None, "tgt"),
        P("grp", "src", None, "tgt"),
        P(("grp", "src"), None, "tgt"),
        P(("grp", "src", "tgt"), None, None, None),
        P(("grp", "src", "tgt"), None),
        P(("grp", "src", "tgt")),
        P(("grp", "src", "tgt"), None),
    )
    return jax.shard_map(
        shards, mesh=mesh, in_specs=placed, out_specs=P("grp", ("src", "tgt")), check_vma=False
    )
```

```python
import functools

import jax
import jax.numpy as jnp
from jax import lax
from jax.experimental import pallas as pl
from jax.experimental.pallas import tpu as pltpu
from jax.sharding import PartitionSpec as P


EXPAND_CHUNKS = 4
UNROLL = 64


def in_vmem():
    return pl.BlockSpec(memory_space=pltpu.VMEM)


def in_smem():
    return pl.BlockSpec(memory_space=pltpu.SMEM)


def in_hbm():
    return pl.BlockSpec(memory_space=pltpu.HBM)


def swapped(value, axis, bit):
    mask = 2**bit
    pairs = [(source, source ^ mask) for source in range(lax.axis_size(axis))]
    return lax.ppermute(value, axis, pairs)


def paired(block):
    half = block.shape[0] // 2
    upper, lower = block[:half], block[half:]
    return jnp.concatenate(
        [jnp.concatenate([upper, -lower], axis=1), jnp.concatenate([lower, upper], axis=1)], axis=0
    )


def partial_kernel(dens_ref, flat_ref, keep_ref, send_ref, total):
    half, rank = keep_ref.shape
    quarter = half // 2
    core = lax.axis_index("tgt")
    product = jnp.dot(dens_ref[...], flat_ref[...], preferred_element_type=jnp.float32)
    total[:half, :] = product[:half, :rank] - product[half:, rank:]
    total[half:, :] = product[:half, rank:] + product[half:, :rank]
    for part in range(2):
        inner = slice(part * quarter, (part + 1) * quarter)
        mine = pl.ds(pl.multiple_of((2 * part + core) * quarter, quarter), quarter)
        other = pl.ds(pl.multiple_of((2 * part + 1 - core) * quarter, quarter), quarter)
        keep_ref[inner, :] = total[mine, :]
        send_ref[inner, :] = total[other, :].astype(send_ref.dtype)


def partial_call(densities, flat):
    rows, points = densities.shape
    rank = flat.shape[1] // 2
    return pl.pallas_call(
        partial_kernel,
        out_shape=(
            jax.ShapeDtypeStruct((rows // 2, rank), jnp.float32),
            jax.ShapeDtypeStruct((rows // 2, rank), jnp.bfloat16),
        ),
        in_specs=[in_vmem(), in_vmem()],
        out_specs=(in_vmem(), in_vmem()),
        scratch_shapes=[pltpu.VMEM((rows, rank), jnp.float32)],
        cost_estimate=pl.CostEstimate(
            flops=4 * rows * points * rank, bytes_accessed=0, transcendentals=0
        ),
        compiler_params=pltpu.CompilerParams(vmem_limit_bytes=16 << 20),
        name="partial",
    )(densities, flat)


def first_kernel(dens_ref, mixed_ref, total, weave):
    clusters = mixed_ref.shape[0]
    width = dens_ref.shape[1] // clusters
    row_id = lax.broadcasted_iota(jnp.int32, weave.shape, 0)
    col_id = lax.broadcasted_iota(jnp.int32, weave.shape, 1)
    goal = jnp.where(row_id < width, 2 * row_id, 2 * (row_id - width) + 1)
    weave[...] = jnp.where(col_id == goal, 1.0, 0.0).astype(jnp.bfloat16)
    for cluster in range(clusters):
        block = paired(dens_ref[:, cluster * width : (cluster + 1) * width])
        woven = jnp.dot(block, weave[...], preferred_element_type=jnp.float32)
        mixed_ref[cluster] = woven.astype(jnp.bfloat16)
    total[...] = jnp.zeros_like(total)


def tiles_kernel(first, last, table_ref, count_ref, mixed_ref, tiles_ref, before, total):
    clusters = mixed_ref.shape[0]
    width = tiles_ref.shape[2]
    count = count_ref[0]
    for start in range(first, last, UNROLL):

        @pl.when(start < count)
        def _():
            table = table_ref[...]
            for slot in range(start, min(start + UNROLL, last)):
                target = jnp.where(slot < count, table[0, slot], clusters)
                columns = pl.ds(pl.multiple_of(target * width, width), width)
                total[:, columns] += jnp.dot(
                    mixed_ref[table[1, slot]], tiles_ref[slot], preferred_element_type=jnp.float32
                )


def first_call(densities, clusters):
    rows, points = densities.shape
    width = points // clusters
    return pl.pallas_call(
        first_kernel,
        out_shape=(
            jax.ShapeDtypeStruct((clusters, rows, 2 * width), jnp.bfloat16),
            jax.ShapeDtypeStruct((rows, points + width), jnp.float32),
        ),
        in_specs=[in_vmem()],
        out_specs=(in_vmem(), in_vmem()),
        scratch_shapes=[pltpu.VMEM((2 * width, 2 * width), jnp.bfloat16)],
        cost_estimate=pl.CostEstimate(
            flops=4 * rows * points * width, bytes_accessed=0, transcendentals=0
        ),
        compiler_params=pltpu.CompilerParams(vmem_limit_bytes=16 << 20),
        name="weave",
    )(densities)


def tiles_call(first, last, table, count, mixed, tiles, total):
    depth, width = tiles.shape[1:]
    return pl.pallas_call(
        functools.partial(tiles_kernel, first, last),
        out_shape=jax.ShapeDtypeStruct(total.shape, total.dtype),
        in_specs=[in_vmem(), in_smem(), in_vmem(), in_vmem(), in_vmem()],
        out_specs=in_vmem(),
        input_output_aliases={4: 0},
        cost_estimate=pl.CostEstimate(
            flops=2 * total.shape[0] * depth * width * (last - first),
            bytes_accessed=0,
            transcendentals=0,
        ),
        compiler_params=pltpu.CompilerParams(vmem_limit_bytes=16 << 20),
        name="tiles",
    )(table, count, mixed, tiles, total)


def far_rows(half, coeff_ref, matrix_ref, near_ref, rows_ref, columns):
    quarter = near_ref.shape[0] // 4
    far = jnp.dot(
        paired(coeff_ref[...]), matrix_ref[:, columns], preferred_element_type=jnp.float32
    )
    for part in range(2):
        source = pl.ds(pl.multiple_of((2 * part + half) * quarter, quarter), quarter)
        inner = slice(part * quarter, (part + 1) * quarter)
        rows_ref[inner, columns] = (far[inner] + near_ref[source, columns]).astype(jnp.bfloat16)


def expand_kernel(flip, order_ref, coeff_ref, matrix_ref, near_ref, *refs):
    out_hbm, rows_ref, sem = refs[-3:]
    quarter = near_ref.shape[0] // 4
    points = matrix_ref.shape[1]
    clusters = order_ref.shape[1]
    width = points // clusters
    core = lax.axis_index("tgt")
    half = 1 - core if flip else core
    order = order_ref[...]
    span = points // EXPAND_CHUNKS
    for chunk in range(EXPAND_CHUNKS):
        columns = slice(chunk * span, (chunk + 1) * span)
        far_rows(half, coeff_ref, matrix_ref, near_ref, rows_ref, columns)
        for cluster in range(
            chunk * clusters // EXPAND_CHUNKS, (chunk + 1) * clusters // EXPAND_CHUNKS
        ):
            place = pl.multiple_of(order[0, cluster] * width, width)
            source = slice(cluster * width, (cluster + 1) * width)
            for part in range(2):
                target = pl.ds(pl.multiple_of((2 * part + half) * quarter, quarter), quarter)
                pltpu.make_async_copy(
                    rows_ref.at[part * quarter : (part + 1) * quarter, source],
                    out_hbm.at[target, pl.ds(place, width)],
                    sem.at[0],
                ).start()
    pltpu.make_async_copy(rows_ref, out_hbm.at[0 : 2 * quarter, :], sem.at[0]).wait()


def expand_call(flip, order, coefficients, matrix, near, result):
    rows = near.shape[0]
    points = matrix.shape[1]
    operands = [order, coefficients, matrix, near]
    specs = [in_vmem()] * 4
    aliases = {}
    if result is not None:
        operands.append(result)
        specs.append(in_hbm())
        aliases = {4: 0}
    return pl.pallas_call(
        functools.partial(expand_kernel, flip),
        out_shape=jax.ShapeDtypeStruct((rows, points), jnp.bfloat16),
        in_specs=specs,
        out_specs=in_hbm(),
        input_output_aliases=aliases,
        scratch_shapes=[
            pltpu.VMEM((rows // 2, points), jnp.bfloat16),
            pltpu.SemaphoreType.DMA((1,)),
        ],
        cost_estimate=pl.CostEstimate(
            flops=4 * coefficients.size * points, bytes_accessed=0, transcendentals=0
        ),
        compiler_params=pltpu.CompilerParams(vmem_limit_bytes=16 << 20),
        name="expand1" if flip else "expand0",
    )(*operands)


def shards(
    densities, compress, level_a, level_b, expand, near_tiles, tile_pairs, tile_count, cluster_order
):
    _, points = densities.shape
    rank = compress.shape[2]
    sections = level_a.shape[0]
    clusters = cluster_order.shape[1]
    width = points // clusters
    slots = near_tiles.shape[0]
    core = lax.axis_index("tgt").astype(jnp.int32)
    tiles = near_tiles.reshape(slots, 2 * width, width)
    ids = jnp.arange(clusters, dtype=jnp.int32)
    found = cluster_order[0][None, :] == tile_pairs[:, 0][:, None]
    places = jnp.sum(jnp.where(found, ids[None, :], 0), axis=1)
    table = jnp.stack([places, tile_pairs[:, 1]])
    count = jnp.minimum(tile_count, slots)
    cut = slots * 3 // 4

    first_core = core == 0
    keep, send = partial_call(densities, compress.reshape(points, 2 * rank))
    arrived = swapped(send, "tgt", 0)
    coefficients = (keep + arrived.astype(jnp.float32)).astype(jnp.bfloat16)

    def both(matrix, earlier):
        planes = matrix.transpose(0, 2, 1, 3)
        other = swapped(planes, "tgt", 0)
        if earlier is not None:
            other, earlier = lax.optimization_barrier((other, earlier))
        joined = jnp.where(
            first_core,
            jnp.concatenate([planes, other], axis=3),
            jnp.concatenate([other, planes], axis=3),
        )
        return joined.reshape(sections, 2 * rank, rank), earlier

    own_matrices, _ = both(level_a, None)
    partner_matrices, own_matrices = both(level_b, own_matrices)
    for section in range(sections):
        partner = swapped(coefficients, "src", section)
        if section == 0:
            mixed, near = first_call(densities, clusters)
        elif section == 1:
            near = tiles_call(0, cut, table, count, mixed, tiles, near)
        elif section == 2:
            near = tiles_call(cut, slots, table, count, mixed, tiles, near)
        own = jnp.dot(
            paired(coefficients), own_matrices[section], preferred_element_type=jnp.float32
        )
        own = lax.optimization_barrier(own)
        updated = own + jnp.dot(
            paired(partner), partner_matrices[section], preferred_element_type=jnp.float32
        )
        coefficients = updated.astype(jnp.bfloat16)
    others = swapped(coefficients, "tgt", 0)
    matrix = expand.transpose(1, 0, 2).reshape(2 * rank, points)
    result = expand_call(False, cluster_order, coefficients, matrix, near, None)
    return expand_call(True, cluster_order, others, matrix, near, result)


def solution(mesh):
    placed = (
        P("grp", ("src", "tgt")),
        P(("grp", "src", "tgt"), None, None),
        P("grp", "src", None, "tgt"),
        P("grp", "src", None, "tgt"),
        P(("grp", "src"), None, "tgt"),
        P(("grp", "src", "tgt"), None, None, None),
        P(("grp", "src", "tgt"), None),
        P(("grp", "src", "tgt")),
        P(("grp", "src", "tgt"), None),
    )
    return jax.shard_map(
        shards, mesh=mesh, in_specs=placed, out_specs=P("grp", ("src", "tgt")), check_vma=False
    )
```

```python
import functools

import jax
import jax.numpy as jnp
from jax import lax
from jax.experimental import pallas as pl
from jax.experimental.pallas import tpu as pltpu
from jax.sharding import PartitionSpec as P


EXPAND_CHUNKS = 8
UNROLL = 64


def in_vmem():
    return pl.BlockSpec(memory_space=pltpu.VMEM)


def in_smem():
    return pl.BlockSpec(memory_space=pltpu.SMEM)


def in_hbm():
    return pl.BlockSpec(memory_space=pltpu.HBM)


def swapped(value, axis, bit):
    mask = 2**bit
    pairs = [(source, source ^ mask) for source in range(lax.axis_size(axis))]
    return lax.ppermute(value, axis, pairs)


def paired(block):
    half = block.shape[0] // 2
    upper, lower = block[:half], block[half:]
    return jnp.concatenate(
        [jnp.concatenate([upper, -lower], axis=1), jnp.concatenate([lower, upper], axis=1)], axis=0
    )


def partial_kernel(dens_ref, flat_ref, keep_ref, send_ref, total):
    half, rank = keep_ref.shape
    quarter = half // 2
    core = lax.axis_index("tgt")
    product = jnp.dot(dens_ref[...], flat_ref[...], preferred_element_type=jnp.float32)
    total[:half, :] = product[:half, :rank] - product[half:, rank:]
    total[half:, :] = product[:half, rank:] + product[half:, :rank]
    for part in range(2):
        inner = slice(part * quarter, (part + 1) * quarter)
        mine = pl.ds(pl.multiple_of((2 * part + core) * quarter, quarter), quarter)
        other = pl.ds(pl.multiple_of((2 * part + 1 - core) * quarter, quarter), quarter)
        keep_ref[inner, :] = total[mine, :]
        send_ref[inner, :] = total[other, :].astype(send_ref.dtype)


def partial_call(densities, flat):
    rows, points = densities.shape
    rank = flat.shape[1] // 2
    return pl.pallas_call(
        partial_kernel,
        out_shape=(
            jax.ShapeDtypeStruct((rows // 2, rank), jnp.float32),
            jax.ShapeDtypeStruct((rows // 2, rank), jnp.bfloat16),
        ),
        in_specs=[in_vmem(), in_vmem()],
        out_specs=(in_vmem(), in_vmem()),
        scratch_shapes=[pltpu.VMEM((rows, rank), jnp.float32)],
        cost_estimate=pl.CostEstimate(
            flops=4 * rows * points * rank, bytes_accessed=0, transcendentals=0
        ),
        compiler_params=pltpu.CompilerParams(vmem_limit_bytes=16 << 20),
        name="partial",
    )(densities, flat)


def first_kernel(dens_ref, mixed_ref, total, weave):
    clusters = mixed_ref.shape[0]
    width = dens_ref.shape[1] // clusters
    row_id = lax.broadcasted_iota(jnp.int32, weave.shape, 0)
    col_id = lax.broadcasted_iota(jnp.int32, weave.shape, 1)
    goal = jnp.where(row_id < width, 2 * row_id, 2 * (row_id - width) + 1)
    weave[...] = jnp.where(col_id == goal, 1.0, 0.0).astype(jnp.bfloat16)
    for cluster in range(clusters):
        block = paired(dens_ref[:, cluster * width : (cluster + 1) * width])
        woven = jnp.dot(block, weave[...], preferred_element_type=jnp.float32)
        mixed_ref[cluster] = woven.astype(jnp.bfloat16)
    total[...] = jnp.zeros_like(total)


def tiles_kernel(first, last, table_ref, count_ref, mixed_ref, tiles_ref, before, *refs):
    fetch = None
    total = refs[0]
    if len(refs) > 1:
        expand_hbm, total, held_ref, sem = refs
        fetch = pltpu.make_async_copy(expand_hbm, held_ref, sem.at[0])
        fetch.start()
    clusters = mixed_ref.shape[0]
    width = tiles_ref.shape[2]
    count = count_ref[0]
    for start in range(first, last, UNROLL):

        @pl.when(start < count)
        def _():
            table = table_ref[...]
            for slot in range(start, min(start + UNROLL, last)):
                target = jnp.where(slot < count, table[0, slot], clusters)
                columns = pl.ds(pl.multiple_of(target * width, width), width)
                total[:, columns] += jnp.dot(
                    mixed_ref[table[1, slot]], tiles_ref[slot], preferred_element_type=jnp.float32
                )
    if fetch is not None:
        fetch.wait()


def first_call(densities, clusters):
    rows, points = densities.shape
    width = points // clusters
    return pl.pallas_call(
        first_kernel,
        out_shape=(
            jax.ShapeDtypeStruct((clusters, rows, 2 * width), jnp.bfloat16),
            jax.ShapeDtypeStruct((rows, points + width), jnp.float32),
        ),
        in_specs=[in_vmem()],
        out_specs=(in_vmem(), in_vmem()),
        scratch_shapes=[pltpu.VMEM((2 * width, 2 * width), jnp.bfloat16)],
        cost_estimate=pl.CostEstimate(
            flops=4 * rows * points * width, bytes_accessed=0, transcendentals=0
        ),
        compiler_params=pltpu.CompilerParams(vmem_limit_bytes=16 << 20),
        name="weave",
    )(densities)


def tiles_call(first, last, table, count, mixed, tiles, total, expand=None):
    depth, width = tiles.shape[1:]
    operands = [table, count, mixed, tiles, total]
    specs = [in_vmem(), in_smem(), in_vmem(), in_vmem(), in_vmem()]
    shapes = [jax.ShapeDtypeStruct(total.shape, total.dtype)]
    scratch = []
    if expand is not None:
        operands.append(pltpu.with_memory_space_constraint(expand, pltpu.HBM))
        specs.append(in_hbm())
        shapes.append(jax.ShapeDtypeStruct(expand.shape, expand.dtype))
        scratch = [pltpu.SemaphoreType.DMA((1,))]
    return pl.pallas_call(
        functools.partial(tiles_kernel, first, last),
        out_shape=tuple(shapes),
        in_specs=specs,
        out_specs=tuple(in_vmem() for _ in shapes),
        input_output_aliases={4: 0},
        scratch_shapes=scratch,
        cost_estimate=pl.CostEstimate(
            flops=2 * total.shape[0] * depth * width * (last - first),
            bytes_accessed=0,
            transcendentals=0,
        ),
        compiler_params=pltpu.CompilerParams(vmem_limit_bytes=16 << 20),
        name="tiles",
    )(*operands)


def far_rows(half, coeff_ref, matrix_ref, near_ref, rows_ref, columns):
    quarter = near_ref.shape[0] // 4
    far = jnp.dot(
        paired(coeff_ref[...]), matrix_ref[:, columns], preferred_element_type=jnp.float32
    )
    for part in range(2):
        source = pl.ds(pl.multiple_of((2 * part + half) * quarter, quarter), quarter)
        inner = slice(part * quarter, (part + 1) * quarter)
        rows_ref[inner, columns] = (far[inner] + near_ref[source, columns]).astype(jnp.bfloat16)


def expand_kernel(flip, order_ref, coeff_ref, matrix_ref, near_ref, *refs):
    out_hbm, rows_ref, sem = refs[-3:]
    quarter = near_ref.shape[0] // 4
    points = matrix_ref.shape[1]
    clusters = order_ref.shape[1]
    width = points // clusters
    core = lax.axis_index("tgt")
    half = 1 - core if flip else core
    order = order_ref[...]
    span = points // EXPAND_CHUNKS
    for chunk in range(EXPAND_CHUNKS):
        columns = slice(chunk * span, (chunk + 1) * span)
        far_rows(half, coeff_ref, matrix_ref, near_ref, rows_ref, columns)
        for cluster in range(
            chunk * clusters // EXPAND_CHUNKS, (chunk + 1) * clusters // EXPAND_CHUNKS
        ):
            place = pl.multiple_of(order[0, cluster] * width, width)
            source = slice(cluster * width, (cluster + 1) * width)
            for part in range(2):
                target = pl.ds(pl.multiple_of((2 * part + half) * quarter, quarter), quarter)
                pltpu.make_async_copy(
                    rows_ref.at[part * quarter : (part + 1) * quarter, source],
                    out_hbm.at[target, pl.ds(place, width)],
                    sem.at[0],
                ).start()
    pltpu.make_async_copy(rows_ref, out_hbm.at[0 : 2 * quarter, :], sem.at[0]).wait()


def expand_call(flip, order, coefficients, matrix, near, result):
    rows = near.shape[0]
    points = matrix.shape[1]
    operands = [order, coefficients, matrix, near]
    specs = [in_vmem()] * 4
    aliases = {}
    if result is not None:
        operands.append(result)
        specs.append(in_hbm())
        aliases = {4: 0}
    return pl.pallas_call(
        functools.partial(expand_kernel, flip),
        out_shape=jax.ShapeDtypeStruct((rows, points), jnp.bfloat16),
        in_specs=specs,
        out_specs=in_hbm(),
        input_output_aliases=aliases,
        scratch_shapes=[
            pltpu.VMEM((rows // 2, points), jnp.bfloat16),
            pltpu.SemaphoreType.DMA((1,)),
        ],
        cost_estimate=pl.CostEstimate(
            flops=4 * coefficients.size * points, bytes_accessed=0, transcendentals=0
        ),
        compiler_params=pltpu.CompilerParams(vmem_limit_bytes=16 << 20),
        name="expand1" if flip else "expand0",
    )(*operands)


def shards(
    densities, compress, level_a, level_b, expand, near_tiles, tile_pairs, tile_count, cluster_order
):
    _, points = densities.shape
    rank = compress.shape[2]
    sections = level_a.shape[0]
    clusters = cluster_order.shape[1]
    width = points // clusters
    slots = near_tiles.shape[0]
    core = lax.axis_index("tgt").astype(jnp.int32)
    tiles = near_tiles.reshape(slots, 2 * width, width)
    ids = jnp.arange(clusters, dtype=jnp.int32)
    found = cluster_order[0][None, :] == tile_pairs[:, 0][:, None]
    places = jnp.sum(jnp.where(found, ids[None, :], 0), axis=1)
    table = jnp.stack([places, tile_pairs[:, 1]])
    count = jnp.minimum(tile_count, slots)
    cut = slots * 2 // 3

    first_core = core == 0
    keep, send = partial_call(densities, compress.reshape(points, 2 * rank))
    arrived = swapped(send, "tgt", 0)
    coefficients = (keep + arrived.astype(jnp.float32)).astype(jnp.bfloat16)

    def both(matrix, earlier):
        planes = matrix.transpose(0, 2, 1, 3)
        other = swapped(planes, "tgt", 0)
        if earlier is not None:
            other, earlier = lax.optimization_barrier((other, earlier))
        joined = jnp.where(
            first_core,
            jnp.concatenate([planes, other], axis=3),
            jnp.concatenate([other, planes], axis=3),
        )
        return joined.reshape(sections, 2 * rank, rank), earlier

    own_matrices, _ = both(level_a, None)
    partner_matrices, own_matrices = both(level_b, own_matrices)
    for section in range(sections):
        partner = swapped(coefficients, "src", section)
        if section == 0:
            mixed, near = first_call(densities, clusters)
        elif section == 1:
            near, held = tiles_call(0, cut, table, count, mixed, tiles, near, expand)
        elif section == 2:
            (near,) = tiles_call(cut, slots, table, count, mixed, tiles, near)
        own = jnp.dot(
            paired(coefficients), own_matrices[section], preferred_element_type=jnp.float32
        )
        own = lax.optimization_barrier(own)
        updated = own + jnp.dot(
            paired(partner), partner_matrices[section], preferred_element_type=jnp.float32
        )
        coefficients = updated.astype(jnp.bfloat16)
    others = swapped(coefficients, "tgt", 0)
    matrix = held.transpose(1, 0, 2).reshape(2 * rank, points)
    result = expand_call(False, cluster_order, coefficients, matrix, near, None)
    return expand_call(True, cluster_order, others, matrix, near, result)


def solution(mesh):
    placed = (
        P("grp", ("src", "tgt")),
        P(("grp", "src", "tgt"), None, None),
        P("grp", "src", None, "tgt"),
        P("grp", "src", None, "tgt"),
        P(("grp", "src"), None, "tgt"),
        P(("grp", "src", "tgt"), None, None, None),
        P(("grp", "src", "tgt"), None),
        P(("grp", "src", "tgt")),
        P(("grp", "src", "tgt"), None),
    )
    return jax.shard_map(
        shards, mesh=mesh, in_specs=placed, out_specs=P("grp", ("src", "tgt")), check_vma=False
    )
```
